32 devices in a mesh: gx: 2 (over x), gy: 4 (over y, core), gz: 4 (over z).
Axes of the slice: x: 2, y: 2, z: 4, core: 2. Of those that a mesh axis runs over, the one named last changes fastest.
Arguments:
- displacement: float32 [3, 64, 128, 512], P(None, 'gz', 'gx', 'gy'), may hold values from -6 to 6
- pressure: float32 [64, 128, 512], P('gz', 'gx', 'gy'), may hold values from -6 to 6
- zone: int32 [64, 128, 512], P('gz', 'gx', 'gy'), may hold values from 0 to 7
- perm_table: float32 [8], replicated, may hold values from 0.2 to 5
- thickness: int32 [128, 512], P('gx', 'gy'), may hold values from 1 to 64, as said below
Outputs:
- heights: float32 [64, 128, 512], P('gz', 'gx', 'gy')
- flow_residual: float32 [64, 128, 512], P('gz', 'gx', 'gy')
- mech_residual: float32 [3, 64, 128, 512], P(None, 'gz', 'gx', 'gy')
The draws below stay inside these ranges and needn't reach their ends.
Inputs may be any that keep to these rules, and one draw needn't show every extreme that they name: Every draw has a column of thickness 64; a rectangular region of the lateral plane holds thick deposit, the rest thin deposit.
All inputs are finite; a program needn't handle non-finite values.
Results may differ from the reference program's by a relative error of at most 0.00002.
Values sent between devices are 32-bit elements; how exact they have to be, the bound alone decides.
A program may use at most 64 MiB of HBM per device.

```python
import math
import jax
import jax.numpy as jnp

ZONES = 8
NZ = 64
NX = 128
NY = 512


def draw_thickness(key, part):
    keys = jax.random.split(key, 4)
    shallow = jax.random.randint(keys[0], (NX, NY), max(1, NZ // 8), NZ // 4 + 1)
    deep = jax.random.randint(keys[1], (NX, NY), 3 * NZ // 4, NZ + 1)
    row_start = jax.random.randint(keys[2], (), 0, NX - NX // 4 + 1)
    col_start = jax.random.randint(keys[3], (), 0, NY - NY // 4 + 1)
    rows = jnp.arange(NX, dtype=jnp.int32)[:, None]
    cols = jnp.arange(NY, dtype=jnp.int32)[None, :]
    inside = (rows >= row_start) & (rows < row_start + NX // 4) & (cols >= col_start) & (cols < col_start + NY // 4)
    result = jnp.where(inside, deep, shallow)
    result = result.at[row_start, col_start].set(NZ)
    return result.astype(jnp.int32)


def set_ends(entries, stream_key, least, largest):
    longest = entries.shape.index(max(entries.shape))
    spots = []
    for shift in (0, 1):
        where = [jax.random.randint(jax.random.fold_in(stream_key, axis), (), 0, length) for axis, length in enumerate(entries.shape)]
        where[longest] = (where[longest] + shift) % entries.shape[longest]
        spots.append(tuple(where))
    return entries.at[spots[0]].set(least).at[spots[1]].set(largest)


def level_of(stream_key, shape, cuts, smallest, top_value):
    loudness, own = 1.0, jax.random.fold_in(stream_key, 6)
    for dim, parts in cuts:
        draws = jnp.exp(jax.random.uniform(jax.random.fold_in(own, dim), (parts,), jnp.float32, smallest / len(cuts), top_value / len(cuts)))
        loudness = loudness * jnp.repeat(draws, shape[dim] // parts).reshape([-1 if axis == dim else 1 for axis in range(len(shape))])
    return loudness


def centred(stream_key, shape, width, reach, shards=(), held_as=jnp.bfloat16):
    entries = jax.random.normal(stream_key, shape, jnp.float32) * width
    if len(shards) > 0:
        entries = level_of(stream_key, shape, shards, -0.22, 0.18) * entries
    return jnp.clip(entries, min=-reach, max=reach).astype(held_as)


def setup_inputs(seed: int = 0) -> dict:
    key_list = jax.random.split(jax.random.key(seed), 6)
    return {
        "displacement": centred(key_list[0], (3, NZ, NX, NY), 1.0, 6.0, ((1, 4), (2, 2), (3, 4)), jnp.float32),
        "pressure": centred(key_list[1], (NZ, NX, NY), 1.0, 6.0, ((0, 4), (1, 2), (2, 4)), jnp.float32),
        "zone": set_ends(jax.random.randint(key_list[2], (NZ, NX, NY), 0, ZONES), jax.random.fold_in(key_list[2], 1), 0, ZONES - 1).astype(jnp.int32),
        "perm_table": jnp.clip(jnp.exp(jax.random.uniform(key_list[3], (ZONES,), jnp.float32, math.log(0.2), math.log(5.0))), 0.2, 5.0),
        "thickness": draw_thickness(jax.random.fold_in(key_list[5], 71), 0),
    }


def take(field, dz, dx, dy):
    return field[..., 1 + dz:field.shape[-3] - 1 + dz, 1 + dx:field.shape[-2] - 1 + dx, 1 + dy:field.shape[-1] - 1 + dy]


def padded(field):
    widths = [(0, 0)] * (field.ndim - 3) + [(1, 1)] * 3
    return jnp.pad(field, widths)


def strain_of(disp_pad):
    div = 0.5 * (take(disp_pad[0], 0, 1, 0) - take(disp_pad[0], 0, -1, 0))
    div = div + 0.5 * (take(disp_pad[1], 0, 0, 1) - take(disp_pad[1], 0, 0, -1))
    div = div + 0.5 * (take(disp_pad[2], 1, 0, 0) - take(disp_pad[2], -1, 0, 0))
    return 0.3 * jnp.tanh(div)


def stencils(disp_pad, press_pad, strain_pad, perm_pad):
    press_mid = take(press_pad, 0, 0, 0)
    perm_mid = take(perm_pad, 0, 0, 0)
    strain_mid = take(strain_pad, 0, 0, 0)
    height_mid = 1.0 + strain_mid
    flow = jnp.zeros_like(press_mid)
    for dz, dx, dy in ((1, 0, 0), (-1, 0, 0), (0, 1, 0), (0, -1, 0), (0, 0, 1), (0, 0, -1)):
        perm_nb = take(perm_pad, dz, dx, dy)
        if dz == 0:
            cond = 2.0 * perm_mid * perm_nb / (perm_mid + perm_nb)
        else:
            height_nb = 1.0 + take(strain_pad, dz, dx, dy)
            cond = 4.0 * perm_mid * perm_nb / ((perm_mid + perm_nb) * (height_mid + height_nb))
        flow = flow + cond * (take(press_pad, dz, dx, dy) - press_mid)
    flow = flow - strain_mid
    disp_mid = take(disp_pad, 0, 0, 0)
    lateral = take(disp_pad, 0, 1, 0) + take(disp_pad, 0, -1, 0) + take(disp_pad, 0, 0, 1) + take(disp_pad, 0, 0, -1) - 4.0 * disp_mid
    height_up = 1.0 + take(strain_pad, 1, 0, 0)
    height_dn = 1.0 + take(strain_pad, -1, 0, 0)
    vertical = 2.0 * (take(disp_pad, 1, 0, 0) - disp_mid) / (height_mid + height_up) - 2.0 * (disp_mid - take(disp_pad, -1, 0, 0)) / (height_mid + height_dn)

    def grads(field):
        return jnp.stack([0.5 * (take(field, 0, 1, 0) - take(field, 0, -1, 0)), 0.5 * (take(field, 0, 0, 1) - take(field, 0, 0, -1)), 0.5 * (take(field, 1, 0, 0) - take(field, -1, 0, 0))])

    mech = lateral + vertical + 0.5 * grads(strain_pad) - grads(press_pad)
    return flow, mech


def reference(displacement, pressure, zone, perm_table, thickness):
    disp_pad = padded(displacement)
    strain = strain_of(disp_pad)
    layer = jnp.arange(NZ, dtype=jnp.int32)[:, None, None]
    active = (layer < thickness[None, :, :]).astype(jnp.float32)
    cell_thick = (1.0 + strain) * active
    prefix = jnp.cumsum(cell_thick, axis=0)
    heights = prefix / NZ
    burden = (prefix[-1][None, :, :] - prefix) / NZ
    zone_perm = jnp.zeros_like(strain)
    for index in range(ZONES):
        zone_perm = zone_perm + jnp.where(zone == index, perm_table[index], jnp.float32(0.0))
    kperm = zone_perm * (1.0 + strain) ** 3 / (1.0 + 2.0 * burden) * (0.001 + 0.999 * active)
    flow, mech = stencils(disp_pad, padded(pressure), padded(strain), padded(kperm))
    return heights, flow, mech
```

```python
import functools

import jax
import jax.numpy as jnp
from jax import lax
from jax.experimental import pallas as pl
from jax.experimental.pallas import tpu as pltpu
from jax.sharding import PartitionSpec as P

MESH = pl.DeviceIdType.MESH
ZONES = 8
AXES = ("gx", "gy", "gz")
PAD = 8
ROWS = 16

X1, Y1, ZU, ZL, ZP, ZN, X2, Y2, ZS, X3, Y3 = range(11)
MESSAGES = 11


def kernel(
    counts, disp, press, zone, table, thick, heights, flow, mech,
    u, p, s, k, zn, th, pre, tot, xs1, xr1, ys1, yr1, xs2, xr2, ys2, yr2, xs3, xr3, ys3, yr3, cs,
    load_sem, send_sem, recv_sem, col_send, col_recv,
):
    depth, width = disp.shape[1], disp.shape[2]
    lanes = disp.shape[3]
    groups = width // 8
    last = PAD + width
    me = {axis: lax.axis_index(axis) for axis in AXES}
    size = dict(zip(AXES, counts))
    depth_total = depth * size["gz"]
    own = pl.ds(PAD, width)
    f32 = jnp.float32

    def has(axis, side):
        return me[axis] > 0 if side == 0 else me[axis] < size[axis] - 1

    def peer(axis, side):
        return {axis: me[axis] + (1 if side else -1)}

    loads = [
        pltpu.make_async_copy(disp.at[1], u.at[1, pl.ds(1, depth), own], load_sem.at[0]),
        pltpu.make_async_copy(disp.at[0], u.at[0, pl.ds(1, depth), own], load_sem.at[1]),
        pltpu.make_async_copy(disp.at[2], u.at[2, pl.ds(1, depth), own], load_sem.at[2]),
        pltpu.make_async_copy(press, p.at[pl.ds(1, depth), own], load_sem.at[3]),
        pltpu.make_async_copy(thick, th, load_sem.at[4]),
        pltpu.make_async_copy(zone, zn.at[pl.ds(1, depth)], load_sem.at[5]),
    ]
    for load in loads:
        load.start()

    barrier = pltpu.get_barrier_semaphore()
    partners = jnp.int32(size["gz"] - 1)
    for axis in ("gx", "gy"):
        for side in (0, 1):
            @pl.when(has(axis, side))
            def _():
                pl.semaphore_signal(barrier, inc=1, device_id=peer(axis, side), device_id_type=MESH)
            partners = partners + has(axis, side).astype(jnp.int32)
    for off in range(1, size["gz"]):
        pl.semaphore_signal(
            barrier, inc=1, device_id={"gz": lax.rem(me["gz"] + off, size["gz"])}, device_id_type=MESH
        )
    pl.semaphore_wait(barrier, partners)

    pending = []

    def copy(message, axis, side, src, dst, at):
        return pltpu.make_async_remote_copy(
            src_ref=src,
            dst_ref=dst,
            send_sem=send_sem.at[message, side],
            recv_sem=recv_sem.at[message, side],
            device_id=peer(axis, at),
            device_id_type=MESH,
        )

    def send(message, axis, srcs, dsts):
        for side in (0, 1):
            @pl.when(has(axis, side))
            def _():
                copy(message, axis, side, srcs[side], dsts[1 - side], side).start()
        pending.append((message, axis, srcs, dsts))

    def receive(message, axis, srcs, dsts):
        for side in (0, 1):
            @pl.when(has(axis, 1 - side))
            def _():
                copy(message, axis, side, srcs[side], dsts[1 - side], 1 - side).wait_recv()

    def clear(axis, refs):
        for side in (0, 1):
            @pl.when(jnp.logical_not(has(axis, side)))
            def _():
                for ref in refs[side]:
                    ref[...] = jnp.zeros(ref.shape, ref.dtype)

    def pair(ref):
        return (ref.at[0], ref.at[1])

    zu = ((disp.at[2, 0], disp.at[2, depth - 1]), (u.at[2, 0, own], u.at[2, depth + 1, own]))
    zl = (
        (disp.at[pl.ds(0, 2), 0], disp.at[pl.ds(0, 2), depth - 1]),
        (u.at[pl.ds(0, 2), 0, own], u.at[pl.ds(0, 2), depth + 1, own]),
    )
    zp = ((press.at[0], press.at[depth - 1]), (p.at[0, own], p.at[depth + 1, own]))
    zz = ((zone.at[0], zone.at[depth - 1]), (zn.at[0], zn.at[depth + 1]))
    zs = ((s.at[1, own], s.at[depth, own]), (s.at[0, own], s.at[depth + 1, own]))
    send(ZU, "gz", *zu)

    lane = lax.broadcasted_iota(jnp.int32, (8, lanes), 1)
    lane_r = lax.broadcasted_iota(jnp.int32, (ROWS, lanes), 1)
    first_lane, last_lane = lane_r == 0, lane_r == lanes - 1
    zero8 = jnp.zeros((8, lanes), f32)

    def pack(values, z, g, lo, hi):
        slot = z * groups + g
        turned = pltpu.roll(values, slot, 1)
        hi = jnp.where(lane == slot, turned, hi)
        lo = jnp.where(lane == lax.rem(slot + lanes - 1, lanes), turned, lo)
        return lo, hi

    def yshift(v, packs, z, row):
        lo, hi = [], []
        lo_pack, hi_pack = packs
        for g in range(ROWS // 8):
            slot = z * groups + row // 8 + g
            lo.append(pltpu.roll(lo_pack, lax.rem(lanes + 1 - slot, lanes), 1))
            hi.append(pltpu.roll(hi_pack, lanes - 1 - slot, 1))
        lo, hi = jnp.concatenate(lo, axis=0), jnp.concatenate(hi, axis=0)
        below = jnp.where(first_lane, lo, pltpu.roll(v, 1, 1))
        above = jnp.where(last_lane, hi, pltpu.roll(v, lanes - 1, 1))
        return below, above

    fields = [u.at[0], u.at[1], u.at[2], p]

    for load in loads[:4]:
        load.wait()

    def pack_inputs(z, accs):
        out = []
        for i, field in enumerate(fields):
            xs1[0, i, z] = field[z + 1, PAD:PAD + 1, :]
            xs1[1, i, z] = field[z + 1, last - 1:last, :]
            lo, hi = accs[2 * i:2 * i + 2]
            for g in range(groups):
                lo, hi = pack(field[z + 1, PAD + 8 * g:PAD + 8 * g + 8, :], z, g, lo, hi)
            out += [lo, hi]
        return tuple(out)

    accs = lax.fori_loop(0, depth, pack_inputs, (zero8,) * 8)
    for i in range(4):
        ys1[0, i] = accs[2 * i + 1]
        ys1[1, i] = accs[2 * i]
    x1, y1 = (pair(xs1), pair(xr1)), (pair(ys1), pair(yr1))
    x2, y2 = (pair(xs2), pair(xr2)), (pair(ys2), pair(yr2))
    x3, y3 = (pair(xs3), pair(xr3)), (pair(ys3), pair(yr3))
    send(X1, "gx", *x1)
    send(Y1, "gy", *y1)
    send(ZL, "gz", *zl)
    send(ZP, "gz", *zp)
    send(ZN, "gz", *zz)

    clear("gx", [[xr.at[side] for xr in (xr1, xr2, xr3)] for side in (0, 1)])
    clear("gy", [[yr.at[side] for yr in (yr1, yr2, yr3)] for side in (0, 1)])
    edges = (0, depth + 1)
    clear("gz", [[u.at[:, z, own], p.at[z, own], s.at[z, own], k.at[z, own], zn.at[z]] for z in edges])
    loads[4].wait()

    receive(ZU, "gz", *zu)
    receive(X1, "gx", *x1)
    receive(Y1, "gy", *y1)

    def unpack_inputs(z, carry):
        for i, field in enumerate(fields):
            field[z + 1, PAD - 1:PAD, :] = xr1[0, i, z]
            field[z + 1, last:last + 1, :] = xr1[1, i, z]
        return carry

    lax.fori_loop(0, depth, unpack_inputs, 0)

    def shifts(field, packs, z, row):
        at = PAD + row
        mid = field[z + 1, at:at + ROWS, :]
        xm = field[z + 1, at - 1:at - 1 + ROWS, :]
        xp = field[z + 1, at + 1:at + 1 + ROWS, :]
        ym, yp = yshift(mid, packs, z, row)
        return mid, xm, xp, ym, yp

    base = me["gz"] * depth
    chunks = range(0, width, ROWS)

    ylo, yhi = zero8, zero8
    for row in chunks:
        rows = slice(row, row + ROWS)
        at = slice(PAD + row, PAD + row + ROWS)
        height = th[rows, :]
        packs = (yr1[0, 1], yr1[1, 1])

        def strain_step(z, carry):
            acc, lo, hi = carry
            up = u[0, z + 1, PAD + row + 1:PAD + row + 1 + ROWS, :]
            down = u[0, z + 1, PAD + row - 1:PAD + row - 1 + ROWS, :]
            ym, yp = yshift(u[1, z + 1, at, :], packs, z, row)
            div = 0.5 * (up - down) + 0.5 * (yp - ym) + 0.5 * (u[2, z + 2, at, :] - u[2, z, at, :])
            st = 0.3 * jnp.tanh(div)
            s[z + 1, at, :] = st
            if row == 0:
                xs2[0, z] = st[0:1, :]
            if row + ROWS == width:
                xs2[1, z] = st[ROWS - 1:ROWS, :]
            for g in range(ROWS // 8):
                lo, hi = pack(st[8 * g:8 * g + 8, :], z, row // 8 + g, lo, hi)
            acc = acc + jnp.where(base + z < height, 1.0 + st, 0.0)
            pre[z, rows, :] = acc
            return acc, lo, hi

        acc, ylo, yhi = lax.fori_loop(0, depth, strain_step, (jnp.zeros((ROWS, lanes), f32), ylo, yhi))
        tot[rows, :] = acc
    ys2[0], ys2[1] = yhi, ylo

    def column(off, at):
        return pltpu.make_async_remote_copy(
            src_ref=tot,
            dst_ref=cs.at[off - 1],
            send_sem=col_send.at[off - 1],
            recv_sem=col_recv.at[off - 1],
            device_id={"gz": lax.rem(me["gz"] + at, size["gz"])},
            device_id_type=MESH,
        )

    for off in range(1, size["gz"]):
        column(off, off).start()
    send(X2, "gx", *x2)
    send(Y2, "gy", *y2)
    send(ZS, "gz", *zs)

    receive(ZP, "gz", *zp)
    for row in chunks:
        rows = slice(row, row + ROWS)
        at = slice(PAD + row, PAD + row + ROWS)
        packs = [(yr1[0, i], yr1[1, i]) for i in range(4)]

        def lateral_step(z, carry):
            _, xm, xp, ym, yp = shifts(p, packs[3], z, row)
            grads = (xp - xm, yp - ym, p[z + 2, at, :] - p[z, at, :])
            for c in range(3):
                mid, xm, xp, ym, yp = shifts(u.at[c], packs[c], z, row)
                mech[c, z, rows, :] = xp + xm + yp + ym - 4.0 * mid - 0.5 * grads[c]
            return carry

        lax.fori_loop(0, depth, lateral_step, 0)

    loads[5].wait()
    for off in range(1, size["gz"]):
        column(off, size["gz"] - off).wait_recv()
    receive(ZS, "gz", *zs)
    receive(ZN, "gz", *zz)

    def permeability(zones, st, burden, active):
        h = 1.0 + st
        perm = jnp.full(zones.shape, table[0], f32)
        for i in range(1, ZONES):
            perm = jnp.where(zones == i, table[i], perm)
        return perm * (h * h * h) / (1.0 + 2.0 * burden) * jnp.where(active, 0.001 + 0.999, 0.001)

    ylo, yhi = zero8, zero8
    for row in chunks:
        rows = slice(row, row + ROWS)
        at = slice(PAD + row, PAD + row + ROWS)
        height = th[rows, :]
        offset = jnp.zeros((ROWS, lanes), f32)
        total = tot[rows, :]
        for off in range(1, size["gz"]):
            piece = cs[off - 1, rows, :]
            lower = (me["gz"] >= off).astype(f32)
            offset = offset + piece * lower
            total = total + piece

        def kperm_step(z, carry):
            lo, hi = carry
            prefix = pre[z, rows, :] + offset
            heights[z, rows, :] = prefix / depth_total
            kp = permeability(
                zn[z + 1, rows, :], s[z + 1, at, :], (total - prefix) / depth_total, base + z < height
            )
            k[z + 1, at, :] = kp
            if row == 0:
                xs3[0, z] = kp[0:1, :]
            if row + ROWS == width:
                xs3[1, z] = kp[ROWS - 1:ROWS, :]
            for g in range(ROWS // 8):
                lo, hi = pack(kp[8 * g:8 * g + 8, :], z, row // 8 + g, lo, hi)
            return lo, hi

        ylo, yhi = lax.fori_loop(0, depth, kperm_step, (ylo, yhi))

        @pl.when(has("gz", 0))
        def _():
            k[0, at, :] = permeability(
                zn[0, rows, :], s[0, at, :], (total - offset) / depth_total, base - 1 < height
            )

        @pl.when(has("gz", 1))
        def _():
            st = s[depth + 1, at, :]
            active = base + depth < height
            prefix = offset + tot[rows, :] + jnp.where(active, 1.0 + st, 0.0)
            k[depth + 1, at, :] = permeability(
                zn[depth + 1, rows, :], st, (total - prefix) / depth_total, active
            )

    ys3[0], ys3[1] = yhi, ylo
    send(X3, "gx", *x3)
    send(Y3, "gy", *y3)

    receive(ZL, "gz", *zl)
    receive(X2, "gx", *x2)
    receive(Y2, "gy", *y2)

    def unpack_strain(z, carry):
        s[z + 1, PAD - 1:PAD, :] = xr2[0, z]
        s[z + 1, last:last + 1, :] = xr2[1, z]
        return carry

    lax.fori_loop(0, depth, unpack_strain, 0)

    for row in chunks:
        rows = slice(row, row + ROWS)
        at = slice(PAD + row, PAD + row + ROWS)
        packs = (yr2[0], yr2[1])

        def faces(z):
            ka, kb = k[z, at, :], k[z + 1, at, :]
            hh = 2.0 + s[z, at, :] + s[z + 1, at, :]
            twice = 2.0 / hh
            cond = 2.0 * twice * (ka * kb) / (ka + kb)
            fluxes = [twice * (u[c, z + 1, at, :] - u[c, z, at, :]) for c in range(3)]
            return fluxes, cond * (p[z + 1, at, :] - p[z, at, :])

        def vertical_step(z, carry):
            below, flow_below = carry
            above, flow_above = faces(z + 1)
            mid, xm, xp, ym, yp = shifts(s, packs, z, row)
            flow[z, rows, :] = flow_above - flow_below - mid
            grads = (xp - xm, yp - ym, s[z + 2, at, :] - s[z, at, :])
            for c in range(3):
                mech[c, z, rows, :] = mech[c, z, rows, :] + (above[c] - below[c]) + 0.25 * grads[c]
            return above, flow_above

        lax.fori_loop(0, depth, vertical_step, faces(0))

    receive(X3, "gx", *x3)
    receive(Y3, "gy", *y3)

    def unpack_kperm(z, carry):
        k[z + 1, PAD - 1:PAD, :] = xr3[0, z]
        k[z + 1, last:last + 1, :] = xr3[1, z]
        return carry

    lax.fori_loop(0, depth, unpack_kperm, 0)
    for row in chunks:
        rows = slice(row, row + ROWS)
        p_packs = (yr1[0, 3], yr1[1, 3])
        k_packs = (yr3[0], yr3[1])

        def flow_step(z, carry):
            ka, *ks = shifts(k, k_packs, z, row)
            pa, *ps = shifts(p, p_packs, z, row)
            out = flow[z, rows, :]
            twice = 2.0 * ka
            for kb, pb in zip(ks, ps):
                out = out + twice * kb / (ka + kb) * (pb - pa)
            flow[z, rows, :] = out
            return carry

        lax.fori_loop(0, depth, flow_step, 0)

    for message, axis, srcs, dsts in pending:
        for side in (0, 1):
            @pl.when(has(axis, side))
            def _():
                copy(message, axis, side, srcs[side], dsts[1 - side], side).wait_send()
    for off in range(1, size["gz"]):
        column(off, off).wait_send()


def local(counts, displacement, pressure, zone, perm_table, thickness):
    _, depth, width, lanes = displacement.shape
    f32 = jnp.float32
    tall = (depth + 2, width + 2 * PAD, lanes)
    row_face = lambda *lead: pltpu.VMEM((2, *lead, depth, 1, lanes), f32)
    lane_face = lambda *lead: pltpu.VMEM((2, *lead, 8, lanes), f32)
    hbm, vmem, smem = (pl.BlockSpec(memory_space=m) for m in (pl.ANY, pltpu.VMEM, pltpu.SMEM))
    others = max(counts[2] - 1, 1)
    return pl.pallas_call(
        functools.partial(kernel, counts),
        out_shape=(
            jax.ShapeDtypeStruct(pressure.shape, f32),
            jax.ShapeDtypeStruct(pressure.shape, f32),
            jax.ShapeDtypeStruct(displacement.shape, f32),
        ),
        in_specs=[hbm, hbm, hbm, smem, hbm],
        out_specs=(vmem, vmem, vmem),
        scratch_shapes=[
            pltpu.VMEM((3, *tall), f32),
            pltpu.VMEM(tall, f32),
            pltpu.VMEM(tall, f32),
            pltpu.VMEM(tall, f32),
            pltpu.VMEM((depth + 2, width, lanes), jnp.int32),
            pltpu.VMEM((width, lanes), jnp.int32),
            pltpu.VMEM((depth, width, lanes), f32),
            pltpu.VMEM((width, lanes), f32),
            row_face(4), row_face(4), lane_face(4), lane_face(4),
            row_face(), row_face(), lane_face(), lane_face(),
            row_face(), row_face(), lane_face(), lane_face(),
            pltpu.VMEM((others, width, lanes), f32),
            pltpu.SemaphoreType.DMA((6,)),
            pltpu.SemaphoreType.DMA((MESSAGES, 2)),
            pltpu.SemaphoreType.DMA((MESSAGES, 2)),
            pltpu.SemaphoreType.DMA((others,)),
            pltpu.SemaphoreType.DMA((others,)),
        ],
        compiler_params=pltpu.CompilerParams(
            collective_id=0, has_side_effects=True, vmem_limit_bytes=40 * 2**20
        ),
    )(displacement, pressure, zone, perm_table, thickness)


def solution(mesh):
    counts = tuple(mesh.shape[axis] for axis in AXES)
    in_specs = (
        P(None, "gz", "gx", "gy"),
        P("gz", "gx", "gy"),
        P("gz", "gx", "gy"),
        P(),
        P("gx", "gy"),
    )
    out_specs = (P("gz", "gx", "gy"), P("gz", "gx", "gy"), P(None, "gz", "gx", "gy"))
    return jax.shard_map(
        functools.partial(local, counts), mesh=mesh, in_specs=in_specs, out_specs=out_specs, check_vma=False
    )
```

```python
import functools

import jax
import jax.numpy as jnp
from jax import lax
from jax.experimental import pallas as pl
from jax.experimental.pallas import tpu as pltpu
from jax.sharding import PartitionSpec as P

MESH = pl.DeviceIdType.MESH
ZONES = 8
AXES = ("gx", "gy", "gz")
PAD = 8
ROWS = 32
UNROLL = 4

X1, Y1, ZU, ZL, ZP, ZN, X2, Y2, ZS, X3, Y3 = range(11)
MESSAGES = 11


def kernel(
    counts, disp, press, zone, table, thick, heights, flow, mech,
    u, p, s, k, zn, th, pre, tot, xs1, xr1, ys1, yr1, xs2, xr2, ys2, yr2, xs3, xr3, ys3, yr3, cs,
    load_sem, send_sem, recv_sem, col_send, col_recv,
):
    depth, width = disp.shape[1], disp.shape[2]
    lanes = disp.shape[3]
    groups = width // 8
    last = PAD + width
    me = {axis: lax.axis_index(axis) for axis in AXES}
    size = dict(zip(AXES, counts))
    depth_total = depth * size["gz"]
    own = pl.ds(PAD, width)
    f32 = jnp.float32

    def has(axis, side):
        return me[axis] > 0 if side == 0 else me[axis] < size[axis] - 1

    def peer(axis, side):
        return {axis: me[axis] + (1 if side else -1)}

    loads = [
        pltpu.make_async_copy(disp.at[1], u.at[1, pl.ds(1, depth), own], load_sem.at[0]),
        pltpu.make_async_copy(disp.at[0], u.at[0, pl.ds(1, depth), own], load_sem.at[1]),
        pltpu.make_async_copy(disp.at[2], u.at[2, pl.ds(1, depth), own], load_sem.at[2]),
        pltpu.make_async_copy(press, p.at[pl.ds(1, depth), own], load_sem.at[3]),
        pltpu.make_async_copy(thick, th, load_sem.at[4]),
        pltpu.make_async_copy(zone, zn.at[pl.ds(1, depth)], load_sem.at[5]),
    ]
    for load in loads:
        load.start()

    barrier = pltpu.get_barrier_semaphore()
    partners = jnp.int32(size["gz"] - 1)
    for axis in ("gx", "gy"):
        for side in (0, 1):
            @pl.when(has(axis, side))
            def _():
                pl.semaphore_signal(barrier, inc=1, device_id=peer(axis, side), device_id_type=MESH)
            partners = partners + has(axis, side).astype(jnp.int32)
    for off in range(1, size["gz"]):
        pl.semaphore_signal(
            barrier, inc=1, device_id={"gz": lax.rem(me["gz"] + off, size["gz"])}, device_id_type=MESH
        )
    pl.semaphore_wait(barrier, partners)

    pending = []

    def copy(message, axis, side, src, dst, at):
        return pltpu.make_async_remote_copy(
            src_ref=src,
            dst_ref=dst,
            send_sem=send_sem.at[message, side],
            recv_sem=recv_sem.at[message, side],
            device_id=peer(axis, at),
            device_id_type=MESH,
        )

    def send(message, axis, srcs, dsts):
        for side in (0, 1):
            @pl.when(has(axis, side))
            def _():
                copy(message, axis, side, srcs[side], dsts[1 - side], side).start()
        pending.append((message, axis, srcs, dsts))

    def receive(message, axis, srcs, dsts):
        for side in (0, 1):
            @pl.when(has(axis, 1 - side))
            def _():
                copy(message, axis, side, srcs[side], dsts[1 - side], 1 - side).wait_recv()

    def clear(axis, refs):
        for side in (0, 1):
            @pl.when(jnp.logical_not(has(axis, side)))
            def _():
                for ref in refs[side]:
                    ref[...] = jnp.zeros(ref.shape, ref.dtype)

    def pair(ref):
        return (ref.at[0], ref.at[1])

    zu = ((disp.at[2, 0], disp.at[2, depth - 1]), (u.at[2, 0, own], u.at[2, depth + 1, own]))
    zl = (
        (disp.at[pl.ds(0, 2), 0], disp.at[pl.ds(0, 2), depth - 1]),
        (u.at[pl.ds(0, 2), 0, own], u.at[pl.ds(0, 2), depth + 1, own]),
    )
    zp = ((press.at[0], press.at[depth - 1]), (p.at[0, own], p.at[depth + 1, own]))
    zz = ((zone.at[0], zone.at[depth - 1]), (zn.at[0], zn.at[depth + 1]))
    zs = ((s.at[1, own], s.at[depth, own]), (s.at[0, own], s.at[depth + 1, own]))
    send(ZU, "gz", *zu)

    lane = lax.broadcasted_iota(jnp.int32, (8, lanes), 1)
    lane_r = lax.broadcasted_iota(jnp.int32, (ROWS, lanes), 1)
    first_lane, last_lane = lane_r == 0, lane_r == lanes - 1
    zero8 = jnp.zeros((8, lanes), f32)

    def pack(values, z, g, lo, hi):
        slot = z * groups + g
        turned = pltpu.roll(values, slot, 1)
        hi = jnp.where(lane == slot, turned, hi)
        lo = jnp.where(lane == lax.rem(slot + lanes - 1, lanes), turned, lo)
        return lo, hi

    def yshift(v, packs, z, row):
        lo, hi = [], []
        lo_pack, hi_pack = packs
        for g in range(ROWS // 8):
            slot = z * groups + row // 8 + g
            lo.append(pltpu.roll(lo_pack, lax.rem(lanes + 1 - slot, lanes), 1))
            hi.append(pltpu.roll(hi_pack, lanes - 1 - slot, 1))
        lo, hi = jnp.concatenate(lo, axis=0), jnp.concatenate(hi, axis=0)
        below = jnp.where(first_lane, lo, pltpu.roll(v, 1, 1))
        above = jnp.where(last_lane, hi, pltpu.roll(v, lanes - 1, 1))
        return below, above

    fields = [u.at[0], u.at[1], u.at[2], p]

    for load in loads[:4]:
        load.wait()

    def pack_inputs(z, accs):
        out = []
        for i, field in enumerate(fields):
            xs1[0, i, z] = field[z + 1, PAD:PAD + 1, :]
            xs1[1, i, z] = field[z + 1, last - 1:last, :]
            lo, hi = accs[2 * i:2 * i + 2]
            for g in range(groups):
                lo, hi = pack(field[z + 1, PAD + 8 * g:PAD + 8 * g + 8, :], z, g, lo, hi)
            out += [lo, hi]
        return tuple(out)

    accs = lax.fori_loop(0, depth, pack_inputs, (zero8,) * 8, unroll=UNROLL)
    for i in range(4):
        ys1[0, i] = accs[2 * i + 1]
        ys1[1, i] = accs[2 * i]
    x1, y1 = (pair(xs1), pair(xr1)), (pair(ys1), pair(yr1))
    x2, y2 = (pair(xs2), pair(xr2)), (pair(ys2), pair(yr2))
    x3, y3 = (pair(xs3), pair(xr3)), (pair(ys3), pair(yr3))
    send(X1, "gx", *x1)
    send(Y1, "gy", *y1)
    send(ZL, "gz", *zl)
    send(ZP, "gz", *zp)
    send(ZN, "gz", *zz)

    clear("gx", [[xr.at[side] for xr in (xr1, xr2, xr3)] for side in (0, 1)])
    clear("gy", [[yr.at[side] for yr in (yr1, yr2, yr3)] for side in (0, 1)])
    edges = (0, depth + 1)
    clear("gz", [[u.at[:, z, own], p.at[z, own], s.at[z, own], k.at[z, own], zn.at[z]] for z in edges])
    loads[4].wait()

    receive(ZU, "gz", *zu)
    receive(X1, "gx", *x1)
    receive(Y1, "gy", *y1)

    def unpack_inputs(z, carry):
        for i, field in enumerate(fields):
            field[z + 1, PAD - 1:PAD, :] = xr1[0, i, z]
            field[z + 1, last:last + 1, :] = xr1[1, i, z]
        return carry

    lax.fori_loop(0, depth, unpack_inputs, 0, unroll=UNROLL)

    def shifts(field, packs, z, row):
        at = PAD + row
        mid = field[z + 1, at:at + ROWS, :]
        xm = field[z + 1, at - 1:at - 1 + ROWS, :]
        xp = field[z + 1, at + 1:at + 1 + ROWS, :]
        ym, yp = yshift(mid, packs, z, row)
        return mid, xm, xp, ym, yp

    base = me["gz"] * depth
    chunks = range(0, width, ROWS)

    ylo, yhi = zero8, zero8
    for row in chunks:
        rows = slice(row, row + ROWS)
        at = slice(PAD + row, PAD + row + ROWS)
        height = th[rows, :]
        packs = (yr1[0, 1], yr1[1, 1])

        def strain_step(z, carry):
            acc, lo, hi = carry
            up = u[0, z + 1, PAD + row + 1:PAD + row + 1 + ROWS, :]
            down = u[0, z + 1, PAD + row - 1:PAD + row - 1 + ROWS, :]
            ym, yp = yshift(u[1, z + 1, at, :], packs, z, row)
            div = 0.5 * (up - down) + 0.5 * (yp - ym) + 0.5 * (u[2, z + 2, at, :] - u[2, z, at, :])
            st = 0.3 * jnp.tanh(div)
            s[z + 1, at, :] = st
            if row == 0:
                xs2[0, z] = st[0:1, :]
            if row + ROWS == width:
                xs2[1, z] = st[ROWS - 1:ROWS, :]
            for g in range(ROWS // 8):
                lo, hi = pack(st[8 * g:8 * g + 8, :], z, row // 8 + g, lo, hi)
            acc = acc + jnp.where(base + z < height, 1.0 + st, 0.0)
            pre[z, rows, :] = acc
            return acc, lo, hi

        acc, ylo, yhi = lax.fori_loop(0, depth, strain_step, (jnp.zeros((ROWS, lanes), f32), ylo, yhi), unroll=UNROLL)
        tot[rows, :] = acc
    ys2[0], ys2[1] = yhi, ylo

    def column(off, at):
        return pltpu.make_async_remote_copy(
            src_ref=tot,
            dst_ref=cs.at[off - 1],
            send_sem=col_send.at[off - 1],
            recv_sem=col_recv.at[off - 1],
            device_id={"gz": lax.rem(me["gz"] + at, size["gz"])},
            device_id_type=MESH,
        )

    for off in range(1, size["gz"]):
        column(off, off).start()
    send(X2, "gx", *x2)
    send(Y2, "gy", *y2)
    send(ZS, "gz", *zs)

    receive(ZP, "gz", *zp)
    for row in chunks:
        rows = slice(row, row + ROWS)
        at = slice(PAD + row, PAD + row + ROWS)
        packs = [(yr1[0, i], yr1[1, i]) for i in range(4)]

        def lateral_step(z, carry):
            _, xm, xp, ym, yp = shifts(p, packs[3], z, row)
            grads = (xp - xm, yp - ym, p[z + 2, at, :] - p[z, at, :])
            for c in range(3):
                mid, xm, xp, ym, yp = shifts(u.at[c], packs[c], z, row)
                mech[c, z, rows, :] = xp + xm + yp + ym - 4.0 * mid - 0.5 * grads[c]
            return carry

        lax.fori_loop(0, depth, lateral_step, 0, unroll=UNROLL)

    loads[5].wait()
    for off in range(1, size["gz"]):
        column(off, size["gz"] - off).wait_recv()
    receive(ZS, "gz", *zs)
    receive(ZN, "gz", *zz)

    def permeability(zones, st, burden, active):
        h = 1.0 + st
        perm = jnp.full(zones.shape, table[0], f32)
        for i in range(1, ZONES):
            perm = jnp.where(zones == i, table[i], perm)
        return perm * (h * h * h) / (1.0 + 2.0 * burden) * jnp.where(active, 0.001 + 0.999, 0.001)

    ylo, yhi = zero8, zero8
    for row in chunks:
        rows = slice(row, row + ROWS)
        at = slice(PAD + row, PAD + row + ROWS)
        height = th[rows, :]
        offset = jnp.zeros((ROWS, lanes), f32)
        total = tot[rows, :]
        for off in range(1, size["gz"]):
            piece = cs[off - 1, rows, :]
            lower = (me["gz"] >= off).astype(f32)
            offset = offset + piece * lower
            total = total + piece

        def kperm_step(z, carry):
            lo, hi = carry
            prefix = pre[z, rows, :] + offset
            heights[z, rows, :] = prefix / depth_total
            kp = permeability(
                zn[z + 1, rows, :], s[z + 1, at, :], (total - prefix) / depth_total, base + z < height
            )
            k[z + 1, at, :] = kp
            if row == 0:
                xs3[0, z] = kp[0:1, :]
            if row + ROWS == width:
                xs3[1, z] = kp[ROWS - 1:ROWS, :]
            for g in range(ROWS // 8):
                lo, hi = pack(kp[8 * g:8 * g + 8, :], z, row // 8 + g, lo, hi)
            return lo, hi

        ylo, yhi = lax.fori_loop(0, depth, kperm_step, (ylo, yhi), unroll=UNROLL)

        @pl.when(has("gz", 0))
        def _():
            k[0, at, :] = permeability(
                zn[0, rows, :], s[0, at, :], (total - offset) / depth_total, base - 1 < height
            )

        @pl.when(has("gz", 1))
        def _():
            st = s[depth + 1, at, :]
            active = base + depth < height
            prefix = offset + tot[rows, :] + jnp.where(active, 1.0 + st, 0.0)
            k[depth + 1, at, :] = permeability(
                zn[depth + 1, rows, :], st, (total - prefix) / depth_total, active
            )

    ys3[0], ys3[1] = yhi, ylo
    send(X3, "gx", *x3)
    send(Y3, "gy", *y3)

    receive(ZL, "gz", *zl)
    receive(X2, "gx", *x2)
    receive(Y2, "gy", *y2)

    def unpack_strain(z, carry):
        s[z + 1, PAD - 1:PAD, :] = xr2[0, z]
        s[z + 1, last:last + 1, :] = xr2[1, z]
        return carry

    lax.fori_loop(0, depth, unpack_strain, 0, unroll=UNROLL)

    for row in chunks:
        rows = slice(row, row + ROWS)
        at = slice(PAD + row, PAD + row + ROWS)
        packs = (yr2[0], yr2[1])

        def faces(z):
            ka, kb = k[z, at, :], k[z + 1, at, :]
            hh = 2.0 + s[z, at, :] + s[z + 1, at, :]
            twice = 2.0 / hh
            cond = 2.0 * twice * (ka * kb) / (ka + kb)
            fluxes = [twice * (u[c, z + 1, at, :] - u[c, z, at, :]) for c in range(3)]
            return fluxes, cond * (p[z + 1, at, :] - p[z, at, :])

        def vertical_step(z, carry):
            below, flow_below = carry
            above, flow_above = faces(z + 1)
            mid, xm, xp, ym, yp = shifts(s, packs, z, row)
            flow[z, rows, :] = flow_above - flow_below - mid
            grads = (xp - xm, yp - ym, s[z + 2, at, :] - s[z, at, :])
            for c in range(3):
                mech[c, z, rows, :] = mech[c, z, rows, :] + (above[c] - below[c]) + 0.25 * grads[c]
            return above, flow_above

        lax.fori_loop(0, depth, vertical_step, faces(0), unroll=UNROLL)

    receive(X3, "gx", *x3)
    receive(Y3, "gy", *y3)

    def unpack_kperm(z, carry):
        k[z + 1, PAD - 1:PAD, :] = xr3[0, z]
        k[z + 1, last:last + 1, :] = xr3[1, z]
        return carry

    lax.fori_loop(0, depth, unpack_kperm, 0, unroll=UNROLL)
    for row in chunks:
        rows = slice(row, row + ROWS)
        p_packs = (yr1[0, 3], yr1[1, 3])
        k_packs = (yr3[0], yr3[1])

        def flow_step(z, carry):
            ka, *ks = shifts(k, k_packs, z, row)
            pa, *ps = shifts(p, p_packs, z, row)
            out = flow[z, rows, :]
            twice = 2.0 * ka
            for kb, pb in zip(ks, ps):
                out = out + twice * kb / (ka + kb) * (pb - pa)
            flow[z, rows, :] = out
            return carry

        lax.fori_loop(0, depth, flow_step, 0, unroll=UNROLL)

    for message, axis, srcs, dsts in pending:
        for side in (0, 1):
            @pl.when(has(axis, side))
            def _():
                copy(message, axis, side, srcs[side], dsts[1 - side], side).wait_send()
    for off in range(1, size["gz"]):
        column(off, off).wait_send()


def store(heights, flow, mech, heights_out, flow_out, mech_out, sem):
    pairs = ((mech, mech_out), (heights, heights_out), (flow, flow_out))
    copies = [pltpu.make_async_copy(src, dst, sem.at[i]) for i, (src, dst) in enumerate(pairs)]
    for copy in copies:
        copy.start()
    for copy in copies:
        copy.wait()


def local(counts, displacement, pressure, zone, perm_table, thickness):
    _, depth, width, lanes = displacement.shape
    f32 = jnp.float32
    tall = (depth + 2, width + 2 * PAD, lanes)
    row_face = lambda *lead: pltpu.VMEM((2, *lead, depth, 1, lanes), f32)
    lane_face = lambda *lead: pltpu.VMEM((2, *lead, 8, lanes), f32)
    hbm, vmem, smem = (pl.BlockSpec(memory_space=m) for m in (pl.ANY, pltpu.VMEM, pltpu.SMEM))
    others = max(counts[2] - 1, 1)
    inputs = [
        pltpu.with_memory_space_constraint(x, pltpu.HBM)
        for x in (displacement, pressure, zone, perm_table, thickness)
    ]
    fields = pl.pallas_call(
        functools.partial(kernel, counts),
        out_shape=(
            pltpu.VMEM(pressure.shape, f32),
            pltpu.VMEM(pressure.shape, f32),
            pltpu.VMEM(displacement.shape, f32),
        ),
        in_specs=[hbm, hbm, hbm, smem, hbm],
        out_specs=(vmem, vmem, vmem),
        scratch_shapes=[
            pltpu.VMEM((3, *tall), f32),
            pltpu.VMEM(tall, f32),
            pltpu.VMEM(tall, f32),
            pltpu.VMEM(tall, f32),
            pltpu.VMEM((depth + 2, width, lanes), jnp.int32),
            pltpu.VMEM((width, lanes), jnp.int32),
            pltpu.VMEM((depth, width, lanes), f32),
            pltpu.VMEM((width, lanes), f32),
            row_face(4), row_face(4), lane_face(4), lane_face(4),
            row_face(), row_face(), lane_face(), lane_face(),
            row_face(), row_face(), lane_face(), lane_face(),
            pltpu.VMEM((others, width, lanes), f32),
            pltpu.SemaphoreType.DMA((6,)),
            pltpu.SemaphoreType.DMA((MESSAGES, 2)),
            pltpu.SemaphoreType.DMA((MESSAGES, 2)),
            pltpu.SemaphoreType.DMA((others,)),
            pltpu.SemaphoreType.DMA((others,)),
        ],
        compiler_params=pltpu.CompilerParams(
            collective_id=0, has_side_effects=True, vmem_limit_bytes=40 * 2**20
        ),
    )(*inputs)
    return pl.pallas_call(
        store,
        out_shape=tuple(jax.ShapeDtypeStruct(x.shape, f32) for x in (pressure, pressure, displacement)),
        in_specs=[vmem] * 3,
        out_specs=(hbm,) * 3,
        scratch_shapes=[pltpu.SemaphoreType.DMA((3,))],
        compiler_params=pltpu.CompilerParams(vmem_limit_bytes=2**20),
    )(*[pltpu.with_memory_space_constraint(x, pltpu.VMEM) for x in fields])


def solution(mesh):
    counts = tuple(mesh.shape[axis] for axis in AXES)
    in_specs = (
        P(None, "gz", "gx", "gy"),
        P("gz", "gx", "gy"),
        P("gz", "gx", "gy"),
        P(),
        P("gx", "gy"),
    )
    out_specs = (P("gz", "gx", "gy"), P("gz", "gx", "gy"), P(None, "gz", "gx", "gy"))
    return jax.shard_map(
        functools.partial(local, counts), mesh=mesh, in_specs=in_specs, out_specs=out_specs, check_vma=False
    )
```

```python
import functools

import jax
import jax.numpy as jnp
from jax import lax
from jax.experimental import pallas as pl
from jax.experimental.pallas import tpu as pltpu
from jax.sharding import PartitionSpec as P

MESH = pl.DeviceIdType.MESH
ZONES = 8
AXES = ("gx", "gy", "gz")
PAD = 8
ROWS = 32
UNROLL = 4

X1, Y1, ZU, ZL, ZP, ZN, X2, Y2, ZS, X3, Y3 = range(11)
MESSAGES = 11


def kernel(
    counts, disp, press, zone, table, thick, heights, flow, mech,
    u, p, s, k, zn, th, pre, tot, xs1, xr1, ys1, yr1, xs2, xr2, ys2, yr2, xs3, xr3, ys3, yr3, cs,
    load_sem, send_sem, recv_sem, col_send, col_recv,
):
    depth, width = disp.shape[1], disp.shape[2]
    lanes = disp.shape[3]
    groups = width // 8
    last = PAD + width
    me = {axis: lax.axis_index(axis) for axis in AXES}
    size = dict(zip(AXES, counts))
    depth_total = depth * size["gz"]
    own = pl.ds(PAD, width)
    f32 = jnp.float32

    def has(axis, side):
        return me[axis] > 0 if side == 0 else me[axis] < size[axis] - 1

    def peer(axis, side):
        return {axis: me[axis] + (1 if side else -1)}

    loads = [
        pltpu.make_async_copy(disp.at[1], u.at[1, pl.ds(1, depth), own], load_sem.at[0]),
        pltpu.make_async_copy(disp.at[0], u.at[0, pl.ds(1, depth), own], load_sem.at[1]),
        pltpu.make_async_copy(disp.at[2], u.at[2, pl.ds(1, depth), own], load_sem.at[2]),
        pltpu.make_async_copy(press, p.at[pl.ds(1, depth), own], load_sem.at[3]),
        pltpu.make_async_copy(thick, th, load_sem.at[4]),
        pltpu.make_async_copy(zone, zn.at[pl.ds(1, depth)], load_sem.at[5]),
    ]
    for load in loads:
        load.start()

    barrier = pltpu.get_barrier_semaphore()
    partners = jnp.int32(size["gz"] - 1)
    for axis in ("gx", "gy"):
        for side in (0, 1):
            @pl.when(has(axis, side))
            def _():
                pl.semaphore_signal(barrier, inc=1, device_id=peer(axis, side), device_id_type=MESH)
            partners = partners + has(axis, side).astype(jnp.int32)
    for off in range(1, size["gz"]):
        pl.semaphore_signal(
            barrier, inc=1, device_id={"gz": lax.rem(me["gz"] + off, size["gz"])}, device_id_type=MESH
        )
    pl.semaphore_wait(barrier, partners)

    pending = []

    def copy(message, axis, side, src, dst, at):
        return pltpu.make_async_remote_copy(
            src_ref=src,
            dst_ref=dst,
            send_sem=send_sem.at[message, side],
            recv_sem=recv_sem.at[message, side],
            device_id=peer(axis, at),
            device_id_type=MESH,
        )

    def send(message, axis, srcs, dsts):
        for side in (0, 1):
            @pl.when(has(axis, side))
            def _():
                copy(message, axis, side, srcs[side], dsts[1 - side], side).start()
        pending.append((message, axis, srcs, dsts))

    def receive(message, axis, srcs, dsts):
        for side in (0, 1):
            @pl.when(has(axis, 1 - side))
            def _():
                copy(message, axis, side, srcs[side], dsts[1 - side], 1 - side).wait_recv()

    def clear(axis, refs):
        for side in (0, 1):
            @pl.when(jnp.logical_not(has(axis, side)))
            def _():
                for ref in refs[side]:
                    ref[...] = jnp.zeros(ref.shape, ref.dtype)

    def pair(ref):
        return (ref.at[0], ref.at[1])

    zu = ((disp.at[2, 0], disp.at[2, depth - 1]), (u.at[2, 0, own], u.at[2, depth + 1, own]))
    zl = (
        (disp.at[pl.ds(0, 2), 0], disp.at[pl.ds(0, 2), depth - 1]),
        (u.at[pl.ds(0, 2), 0, own], u.at[pl.ds(0, 2), depth + 1, own]),
    )
    zp = ((press.at[0], press.at[depth - 1]), (p.at[0, own], p.at[depth + 1, own]))
    zz = ((zone.at[0], zone.at[depth - 1]), (zn.at[0], zn.at[depth + 1]))
    zs = ((s.at[1, own], s.at[depth, own]), (s.at[0, own], s.at[depth + 1, own]))
    send(ZU, "gz", *zu)

    lane = lax.broadcasted_iota(jnp.int32, (8, lanes), 1)
    lane_r = lax.broadcasted_iota(jnp.int32, (ROWS, lanes), 1)
    first_lane, last_lane = lane_r == 0, lane_r == lanes - 1
    zero8 = jnp.zeros((8, lanes), f32)

    def pack(values, z, g, lo, hi):
        slot = z * groups + g
        turned = pltpu.roll(values, slot, 1)
        hi = jnp.where(lane == slot, turned, hi)
        lo = jnp.where(lane == lax.rem(slot + lanes - 1, lanes), turned, lo)
        return lo, hi

    def yshift(v, packs, z, row):
        if packs is None:
            below = jnp.where(first_lane, 0.0, pltpu.roll(v, 1, 1))
            return below, jnp.where(last_lane, 0.0, pltpu.roll(v, lanes - 1, 1))
        lo, hi = [], []
        lo_pack, hi_pack = packs
        for g in range(ROWS // 8):
            slot = z * groups + row // 8 + g
            lo.append(pltpu.roll(lo_pack, lax.rem(lanes + 1 - slot, lanes), 1))
            hi.append(pltpu.roll(hi_pack, lanes - 1 - slot, 1))
        lo, hi = jnp.concatenate(lo, axis=0), jnp.concatenate(hi, axis=0)
        below = jnp.where(first_lane, lo, pltpu.roll(v, 1, 1))
        above = jnp.where(last_lane, hi, pltpu.roll(v, lanes - 1, 1))
        return below, above

    fields = [u.at[0], u.at[1], u.at[2], p]

    for load in loads[:4]:
        load.wait()

    def pack_inputs(z, accs):
        out = []
        for i, field in enumerate(fields):
            xs1[0, i, z] = field[z + 1, PAD:PAD + 1, :]
            xs1[1, i, z] = field[z + 1, last - 1:last, :]
            lo, hi = accs[2 * i:2 * i + 2]
            for g in range(groups):
                lo, hi = pack(field[z + 1, PAD + 8 * g:PAD + 8 * g + 8, :], z, g, lo, hi)
            out += [lo, hi]
        return tuple(out)

    accs = lax.fori_loop(0, depth, pack_inputs, (zero8,) * 8, unroll=UNROLL)
    for i in range(4):
        ys1[0, i] = accs[2 * i + 1]
        ys1[1, i] = accs[2 * i]
    x1, y1 = (pair(xs1), pair(xr1)), (pair(ys1), pair(yr1))
    x2, y2 = (pair(xs2), pair(xr2)), (pair(ys2), pair(yr2))
    x3, y3 = (pair(xs3), pair(xr3)), (pair(ys3), pair(yr3))
    send(X1, "gx", *x1)
    send(Y1, "gy", *y1)
    send(ZL, "gz", *zl)
    send(ZP, "gz", *zp)
    send(ZN, "gz", *zz)

    clear("gx", [[xr.at[side] for xr in (xr1, xr2, xr3)] for side in (0, 1)])
    clear("gy", [[yr.at[side] for yr in (yr1, yr2, yr3)] for side in (0, 1)])
    edges = (0, depth + 1)
    clear("gz", [[u.at[:, z, own], p.at[z, own], s.at[z, own], k.at[z, own], zn.at[z]] for z in edges])
    loads[4].wait()

    receive(ZU, "gz", *zu)
    receive(X1, "gx", *x1)
    receive(Y1, "gy", *y1)

    def unpack_inputs(z, carry):
        for i, field in enumerate(fields):
            field[z + 1, PAD - 1:PAD, :] = xr1[0, i, z]
            field[z + 1, last:last + 1, :] = xr1[1, i, z]
        k[z + 1, PAD - 1:PAD, :] = jnp.zeros((1, lanes), f32)
        k[z + 1, last:last + 1, :] = jnp.zeros((1, lanes), f32)
        return carry

    lax.fori_loop(0, depth, unpack_inputs, 0, unroll=UNROLL)

    def shifts(field, packs, z, row):
        at = PAD + row
        mid = field[z + 1, at:at + ROWS, :]
        xm = field[z + 1, at - 1:at - 1 + ROWS, :]
        xp = field[z + 1, at + 1:at + 1 + ROWS, :]
        ym, yp = yshift(mid, packs, z, row)
        return mid, xm, xp, ym, yp

    base = me["gz"] * depth
    chunks = range(0, width, ROWS)

    ylo, yhi = zero8, zero8
    for row in chunks:
        rows = slice(row, row + ROWS)
        at = slice(PAD + row, PAD + row + ROWS)
        height = th[rows, :]
        packs = (yr1[0, 1], yr1[1, 1])

        def strain_step(z, carry):
            acc, lo, hi = carry
            up = u[0, z + 1, PAD + row + 1:PAD + row + 1 + ROWS, :]
            down = u[0, z + 1, PAD + row - 1:PAD + row - 1 + ROWS, :]
            ym, yp = yshift(u[1, z + 1, at, :], packs, z, row)
            div = 0.5 * (up - down) + 0.5 * (yp - ym) + 0.5 * (u[2, z + 2, at, :] - u[2, z, at, :])
            st = 0.3 * jnp.tanh(div)
            s[z + 1, at, :] = st
            if row == 0:
                xs2[0, z] = st[0:1, :]
            if row + ROWS == width:
                xs2[1, z] = st[ROWS - 1:ROWS, :]
            for g in range(ROWS // 8):
                lo, hi = pack(st[8 * g:8 * g + 8, :], z, row // 8 + g, lo, hi)
            acc = acc + jnp.where(base + z < height, 1.0 + st, 0.0)
            pre[z, rows, :] = acc
            return acc, lo, hi

        acc, ylo, yhi = lax.fori_loop(0, depth, strain_step, (jnp.zeros((ROWS, lanes), f32), ylo, yhi), unroll=UNROLL)
        tot[rows, :] = acc
    ys2[0], ys2[1] = yhi, ylo

    def column(off, at):
        return pltpu.make_async_remote_copy(
            src_ref=tot,
            dst_ref=cs.at[off - 1],
            send_sem=col_send.at[off - 1],
            recv_sem=col_recv.at[off - 1],
            device_id={"gz": lax.rem(me["gz"] + at, size["gz"])},
            device_id_type=MESH,
        )

    for off in range(1, size["gz"]):
        column(off, off).start()
    send(X2, "gx", *x2)
    send(Y2, "gy", *y2)
    send(ZS, "gz", *zs)

    receive(ZP, "gz", *zp)
    for row in chunks:
        rows = slice(row, row + ROWS)
        at = slice(PAD + row, PAD + row + ROWS)
        packs = [(yr1[0, i], yr1[1, i]) for i in range(4)]

        def lateral_step(z, carry):
            _, xm, xp, ym, yp = shifts(p, packs[3], z, row)
            grads = (xp - xm, yp - ym, p[z + 2, at, :] - p[z, at, :])
            for c in range(3):
                mid, xm, xp, ym, yp = shifts(u.at[c], packs[c], z, row)
                mech[c, z, rows, :] = xp + xm + yp + ym - 4.0 * mid - 0.5 * grads[c]
            return carry

        lax.fori_loop(0, depth, lateral_step, 0, unroll=UNROLL)

    loads[5].wait()

    def unloaded(zones, st, active):
        h = 1.0 + st
        perm = jnp.full(zones.shape, table[0], f32)
        for i in range(1, ZONES):
            perm = jnp.where(zones == i, table[i], perm)
        return perm * (h * h * h) * jnp.where(active, 0.001 + 0.999, 0.001)

    for row in chunks:
        rows = slice(row, row + ROWS)
        at = slice(PAD + row, PAD + row + ROWS)
        height = th[rows, :]

        def unloaded_step(z, carry):
            k[z + 1, at, :] = unloaded(zn[z + 1, rows, :], s[z + 1, at, :], base + z < height)
            return carry

        lax.fori_loop(0, depth, unloaded_step, 0, unroll=UNROLL)

    for off in range(1, size["gz"]):
        column(off, size["gz"] - off).wait_recv()

    def column_ends(rows):
        offset = jnp.zeros((ROWS, lanes), f32)
        total = tot[rows, :]
        for off in range(1, size["gz"]):
            piece = cs[off - 1, rows, :]
            offset = offset + piece * (me["gz"] >= off).astype(f32)
            total = total + piece
        return offset, total

    def permeability(free, burden):
        return free / (1.0 + 2.0 * burden)

    ylo, yhi = zero8, zero8
    for row in chunks:
        rows = slice(row, row + ROWS)
        at = slice(PAD + row, PAD + row + ROWS)
        offset, total = column_ends(rows)

        def kperm_step(z, carry):
            lo, hi = carry
            prefix = pre[z, rows, :] + offset
            heights[z, rows, :] = prefix / depth_total
            kp = permeability(k[z + 1, at, :], (total - prefix) / depth_total)
            k[z + 1, at, :] = kp
            if row == 0:
                xs3[0, z] = kp[0:1, :]
            if row + ROWS == width:
                xs3[1, z] = kp[ROWS - 1:ROWS, :]
            for g in range(ROWS // 8):
                lo, hi = pack(kp[8 * g:8 * g + 8, :], z, row // 8 + g, lo, hi)
            return lo, hi

        ylo, yhi = lax.fori_loop(0, depth, kperm_step, (ylo, yhi), unroll=UNROLL)

    ys3[0], ys3[1] = yhi, ylo
    send(X3, "gx", *x3)
    send(Y3, "gy", *y3)

    receive(ZS, "gz", *zs)
    receive(ZN, "gz", *zz)
    for row in chunks:
        rows = slice(row, row + ROWS)
        at = slice(PAD + row, PAD + row + ROWS)
        height = th[rows, :]
        offset, total = column_ends(rows)

        @pl.when(has("gz", 0))
        def _():
            free = unloaded(zn[0, rows, :], s[0, at, :], base - 1 < height)
            k[0, at, :] = permeability(free, (total - offset) / depth_total)

        @pl.when(has("gz", 1))
        def _():
            st = s[depth + 1, at, :]
            active = base + depth < height
            prefix = offset + tot[rows, :] + jnp.where(active, 1.0 + st, 0.0)
            free = unloaded(zn[depth + 1, rows, :], st, active)
            k[depth + 1, at, :] = permeability(free, (total - prefix) / depth_total)

    for row in chunks:
        rows = slice(row, row + ROWS)

        def flow_step(z, carry):
            ka, *ks = shifts(k, None, z, row)
            pa, *ps = shifts(p, None, z, row)
            out = jnp.zeros((ROWS, lanes), f32)
            twice = 2.0 * ka
            for kb, pb in zip(ks, ps):
                out = out + twice * kb / (ka + kb) * (pb - pa)
            flow[z, rows, :] = out
            return carry

        lax.fori_loop(0, depth, flow_step, 0, unroll=UNROLL)

    receive(ZL, "gz", *zl)
    receive(X2, "gx", *x2)
    receive(Y2, "gy", *y2)

    def unpack_strain(z, carry):
        s[z + 1, PAD - 1:PAD, :] = xr2[0, z]
        s[z + 1, last:last + 1, :] = xr2[1, z]
        return carry

    lax.fori_loop(0, depth, unpack_strain, 0, unroll=UNROLL)

    for row in chunks:
        rows = slice(row, row + ROWS)
        at = slice(PAD + row, PAD + row + ROWS)
        packs = (yr2[0], yr2[1])

        def faces(z):
            ka, kb = k[z, at, :], k[z + 1, at, :]
            hh = 2.0 + s[z, at, :] + s[z + 1, at, :]
            twice = 2.0 / hh
            cond = 2.0 * twice * (ka * kb) / (ka + kb)
            fluxes = [twice * (u[c, z + 1, at, :] - u[c, z, at, :]) for c in range(3)]
            return fluxes, cond * (p[z + 1, at, :] - p[z, at, :])

        def vertical_step(z, carry):
            below, flow_below = carry
            above, flow_above = faces(z + 1)
            mid, xm, xp, ym, yp = shifts(s, packs, z, row)
            flow[z, rows, :] = flow[z, rows, :] + (flow_above - flow_below) - mid
            grads = (xp - xm, yp - ym, s[z + 2, at, :] - s[z, at, :])
            for c in range(3):
                mech[c, z, rows, :] = mech[c, z, rows, :] + (above[c] - below[c]) + 0.25 * grads[c]
            return above, flow_above

        lax.fori_loop(0, depth, vertical_step, faces(0), unroll=UNROLL)

    receive(X3, "gx", *x3)
    receive(Y3, "gy", *y3)

    def crossing(ka, kb, pa, pb):
        return 2.0 * ka * kb / (ka + kb) * (pb - pa)

    turn = lambda face: pltpu.roll(face, 1, 1)
    side_lo = crossing(ys3[0], turn(yr3[0]), ys1[0, 3], turn(yr1[0, 3]))
    side_hi = crossing(turn(ys3[1]), yr3[1], turn(ys1[1, 3]), yr1[1, 3])
    first8, last8 = lane == 0, lane == lanes - 1

    def sides_step(z, carry):
        for side, row in ((0, 0), (1, width - 1)):
            out = crossing(xs3[side, z], xr3[side, z], xs1[side, 3, z], xr1[side, 3, z])
            flow[z, row:row + 1, :] = flow[z, row:row + 1, :] + out
        for g in range(groups):
            slot = z * groups + g
            lo = pltpu.roll(side_lo, lax.rem(lanes - slot, lanes), 1)
            hi = pltpu.roll(side_hi, lanes - 1 - slot, 1)
            rows = slice(8 * g, 8 * g + 8)
            flow[z, rows, :] = flow[z, rows, :] + jnp.where(first8, lo, jnp.where(last8, hi, 0.0))
        return carry

    lax.fori_loop(0, depth, sides_step, 0, unroll=UNROLL)

    for message, axis, srcs, dsts in pending:
        for side in (0, 1):
            @pl.when(has(axis, side))
            def _():
                copy(message, axis, side, srcs[side], dsts[1 - side], side).wait_send()
    for off in range(1, size["gz"]):
        column(off, off).wait_send()


def store(heights, flow, mech, heights_out, flow_out, mech_out, sem):
    pairs = ((mech, mech_out), (heights, heights_out), (flow, flow_out))
    copies = [pltpu.make_async_copy(src, dst, sem.at[i]) for i, (src, dst) in enumerate(pairs)]
    for copy in copies:
        copy.start()
    for copy in copies:
        copy.wait()


def local(counts, displacement, pressure, zone, perm_table, thickness):
    _, depth, width, lanes = displacement.shape
    f32 = jnp.float32
    tall = (depth + 2, width + 2 * PAD, lanes)
    row_face = lambda *lead: pltpu.VMEM((2, *lead, depth, 1, lanes), f32)
    lane_face = lambda *lead: pltpu.VMEM((2, *lead, 8, lanes), f32)
    hbm, vmem, smem = (pl.BlockSpec(memory_space=m) for m in (pl.ANY, pltpu.VMEM, pltpu.SMEM))
    others = max(counts[2] - 1, 1)
    inputs = [
        pltpu.with_memory_space_constraint(x, pltpu.HBM)
        for x in (displacement, pressure, zone, perm_table, thickness)
    ]
    fields = pl.pallas_call(
        functools.partial(kernel, counts),
        out_shape=(
            pltpu.VMEM(pressure.shape, f32),
            pltpu.VMEM(pressure.shape, f32),
            pltpu.VMEM(displacement.shape, f32),
        ),
        in_specs=[hbm, hbm, hbm, smem, hbm],
        out_specs=(vmem, vmem, vmem),
        scratch_shapes=[
            pltpu.VMEM((3, *tall), f32),
            pltpu.VMEM(tall, f32),
            pltpu.VMEM(tall, f32),
            pltpu.VMEM(tall, f32),
            pltpu.VMEM((depth + 2, width, lanes), jnp.int32),
            pltpu.VMEM((width, lanes), jnp.int32),
            pltpu.VMEM((depth, width, lanes), f32),
            pltpu.VMEM((width, lanes), f32),
            row_face(4), row_face(4), lane_face(4), lane_face(4),
            row_face(), row_face(), lane_face(), lane_face(),
            row_face(), row_face(), lane_face(), lane_face(),
            pltpu.VMEM((others, width, lanes), f32),
            pltpu.SemaphoreType.DMA((6,)),
            pltpu.SemaphoreType.DMA((MESSAGES, 2)),
            pltpu.SemaphoreType.DMA((MESSAGES, 2)),
            pltpu.SemaphoreType.DMA((others,)),
            pltpu.SemaphoreType.DMA((others,)),
        ],
        compiler_params=pltpu.CompilerParams(
            collective_id=0, has_side_effects=True, vmem_limit_bytes=40 * 2**20
        ),
    )(*inputs)
    return pl.pallas_call(
        store,
        out_shape=tuple(jax.ShapeDtypeStruct(x.shape, f32) for x in (pressure, pressure, displacement)),
        in_specs=[vmem] * 3,
        out_specs=(hbm,) * 3,
        scratch_shapes=[pltpu.SemaphoreType.DMA((3,))],
        compiler_params=pltpu.CompilerParams(vmem_limit_bytes=2**20),
    )(*[pltpu.with_memory_space_constraint(x, pltpu.VMEM) for x in fields])


def solution(mesh):
    counts = tuple(mesh.shape[axis] for axis in AXES)
    in_specs = (
        P(None, "gz", "gx", "gy"),
        P("gz", "gx", "gy"),
        P("gz", "gx", "gy"),
        P(),
        P("gx", "gy"),
    )
    out_specs = (P("gz", "gx", "gy"), P("gz", "gx", "gy"), P(None, "gz", "gx", "gy"))
    return jax.shard_map(
        functools.partial(local, counts), mesh=mesh, in_specs=in_specs, out_specs=out_specs, check_vma=False
    )
```

```python
import functools

import jax
import jax.numpy as jnp
from jax import lax
from jax.experimental import pallas as pl
from jax.experimental.pallas import tpu as pltpu
from jax.sharding import PartitionSpec as P

MESH = pl.DeviceIdType.MESH
ZONES = 8
AXES = ("gx", "gy", "gz")
PAD = 8
ROWS = 32
UNROLL = 8

X0, Y0, X1, Y1, ZU, ZL, ZP, ZN, X2, Y2, ZS, X3, Y3 = range(13)
MESSAGES = 13


def kernel(
    counts, disp, press, zone, table, thick, heights, flow, mech,
    u, p, s, k, zn, th, pre, tot, xs1, xr1, ys1, yr1, ysr, yrr, xs2, xr2, ys2, yr2, xs3, xr3, ys3, yr3, cs,
    load_sem, send_sem, recv_sem, col_send, col_recv,
):
    depth, width = disp.shape[1], disp.shape[2]
    lanes = disp.shape[3]
    groups = width // 8
    last = PAD + width
    me = {axis: lax.axis_index(axis) for axis in AXES}
    size = dict(zip(AXES, counts))
    depth_total = depth * size["gz"]
    own = pl.ds(PAD, width)
    f32 = jnp.float32

    def has(axis, side):
        return me[axis] > 0 if side == 0 else me[axis] < size[axis] - 1

    def peer(axis, side):
        return {axis: me[axis] + (1 if side else -1)}

    loads = [
        pltpu.make_async_copy(disp.at[1], u.at[1, pl.ds(1, depth), own], load_sem.at[0]),
        pltpu.make_async_copy(disp.at[0], u.at[0, pl.ds(1, depth), own], load_sem.at[1]),
        pltpu.make_async_copy(disp.at[2], u.at[2, pl.ds(1, depth), own], load_sem.at[2]),
        pltpu.make_async_copy(press, p.at[pl.ds(1, depth), own], load_sem.at[3]),
        pltpu.make_async_copy(thick, th, load_sem.at[4]),
        pltpu.make_async_copy(zone, zn.at[pl.ds(1, depth)], load_sem.at[5]),
    ]
    for load in loads:
        load.start()

    barrier = pltpu.get_barrier_semaphore()
    partners = jnp.int32(size["gz"] - 1)
    for axis in ("gx", "gy"):
        for side in (0, 1):
            @pl.when(has(axis, side))
            def _():
                pl.semaphore_signal(barrier, inc=1, device_id=peer(axis, side), device_id_type=MESH)
            partners = partners + has(axis, side).astype(jnp.int32)
    for off in range(1, size["gz"]):
        pl.semaphore_signal(
            barrier, inc=1, device_id={"gz": lax.rem(me["gz"] + off, size["gz"])}, device_id_type=MESH
        )

    pending = []

    def copy(message, axis, side, src, dst, at):
        return pltpu.make_async_remote_copy(
            src_ref=src,
            dst_ref=dst,
            send_sem=send_sem.at[message, side],
            recv_sem=recv_sem.at[message, side],
            device_id=peer(axis, at),
            device_id_type=MESH,
        )

    def send(message, axis, srcs, dsts):
        for side in (0, 1):
            @pl.when(has(axis, side))
            def _():
                copy(message, axis, side, srcs[side], dsts[1 - side], side).start()
        pending.append((message, axis, srcs, dsts))

    def receive(message, axis, srcs, dsts):
        for side in (0, 1):
            @pl.when(has(axis, 1 - side))
            def _():
                copy(message, axis, side, srcs[side], dsts[1 - side], 1 - side).wait_recv()

    def clear(axis, refs):
        for side in (0, 1):
            @pl.when(jnp.logical_not(has(axis, side)))
            def _():
                for ref in refs[side]:
                    ref[...] = jnp.zeros(ref.shape, ref.dtype)

    def pair(ref):
        return (ref.at[0], ref.at[1])

    zu = ((disp.at[2, 0], disp.at[2, depth - 1]), (u.at[2, 0, own], u.at[2, depth + 1, own]))
    zl = (
        (disp.at[pl.ds(0, 2), 0], disp.at[pl.ds(0, 2), depth - 1]),
        (u.at[pl.ds(0, 2), 0, own], u.at[pl.ds(0, 2), depth + 1, own]),
    )
    zp = ((press.at[0], press.at[depth - 1]), (p.at[0, own], p.at[depth + 1, own]))
    zz = ((zone.at[0], zone.at[depth - 1]), (zn.at[0], zn.at[depth + 1]))
    zs = ((s.at[1, own], s.at[depth, own]), (s.at[0, own], s.at[depth + 1, own]))
    lane = lax.broadcasted_iota(jnp.int32, (8, lanes), 1)
    lane_r = lax.broadcasted_iota(jnp.int32, (ROWS, lanes), 1)
    first_lane, last_lane = lane_r == 0, lane_r == lanes - 1
    zero8 = jnp.zeros((8, lanes), f32)

    def pack(values, z, g, lo, hi):
        slot = z * groups + g
        turned = pltpu.roll(values, slot, 1)
        hi = jnp.where(lane == slot, turned, hi)
        lo = jnp.where(lane == lax.rem(slot + lanes - 1, lanes), turned, lo)
        return lo, hi

    def yshift(v, packs, z, row):
        if packs is None:
            below = jnp.where(first_lane, 0.0, pltpu.roll(v, 1, 1))
            return below, jnp.where(last_lane, 0.0, pltpu.roll(v, lanes - 1, 1))
        lo, hi = [], []
        lo_pack, hi_pack = packs
        for g in range(ROWS // 8):
            slot = z * groups + row // 8 + g
            lo.append(pltpu.roll(lo_pack, lax.rem(lanes + 1 - slot, lanes), 1))
            hi.append(pltpu.roll(hi_pack, lanes - 1 - slot, 1))
        lo, hi = jnp.concatenate(lo, axis=0), jnp.concatenate(hi, axis=0)
        below = jnp.where(first_lane, lo, pltpu.roll(v, 1, 1))
        above = jnp.where(last_lane, hi, pltpu.roll(v, lanes - 1, 1))
        return below, above

    fields = [u.at[0], u.at[1], u.at[2], p]

    def pack_first(z, carry):
        lo, hi = carry
        xs1[0, 0, z] = u[0, z + 1, PAD:PAD + 1, :]
        xs1[1, 0, z] = u[0, z + 1, last - 1:last, :]
        for g in range(groups):
            lo, hi = pack(u[1, z + 1, PAD + 8 * g:PAD + 8 * g + 8, :], z, g, lo, hi)
        return lo, hi

    loads[0].wait()
    loads[1].wait()
    lo, hi = lax.fori_loop(0, depth, pack_first, (zero8,) * 2, unroll=UNROLL)
    ys1[0] = hi
    ys1[1] = lo

    def part(ref, which):
        return (ref.at[0, which], ref.at[1, which])

    x0, y0 = (part(xs1, 0), part(xr1, 0)), (pair(ys1), pair(yr1))
    x1, y1 = (part(xs1, pl.ds(1, 3)), part(xr1, pl.ds(1, 3))), (pair(ysr), pair(yrr))
    pl.semaphore_wait(barrier, partners)
    send(ZU, "gz", *zu)
    send(X0, "gx", *x0)
    send(Y0, "gy", *y0)

    others = ((0, 0), (2, 1), (3, 2))

    def pack_inputs(z, accs):
        out = []
        for i in range(1, 4):
            xs1[0, i, z] = fields[i][z + 1, PAD:PAD + 1, :]
            xs1[1, i, z] = fields[i][z + 1, last - 1:last, :]
        for i, n in others:
            lo, hi = accs[2 * n:2 * n + 2]
            for g in range(groups):
                lo, hi = pack(fields[i][z + 1, PAD + 8 * g:PAD + 8 * g + 8, :], z, g, lo, hi)
            out += [lo, hi]
        return tuple(out)

    loads[2].wait()
    loads[3].wait()
    accs = lax.fori_loop(0, depth, pack_inputs, (zero8,) * 6, unroll=UNROLL)
    for i, n in others:
        ysr[0, n] = accs[2 * n + 1]
        ysr[1, n] = accs[2 * n]
    x2, y2 = (pair(xs2), pair(xr2)), (pair(ys2), pair(yr2))
    x3, y3 = (pair(xs3), pair(xr3)), (pair(ys3), pair(yr3))
    send(X1, "gx", *x1)
    send(Y1, "gy", *y1)
    send(ZL, "gz", *zl)
    send(ZP, "gz", *zp)
    send(ZN, "gz", *zz)

    clear("gx", [[xr.at[side] for xr in (xr1, xr2, xr3)] for side in (0, 1)])
    clear("gy", [[yr.at[side] for yr in (yr1, yrr, yr2, yr3)] for side in (0, 1)])
    edges = (0, depth + 1)
    clear("gz", [[u.at[:, z, own], p.at[z, own], s.at[z, own], k.at[z, own], zn.at[z]] for z in edges])
    loads[4].wait()

    receive(ZU, "gz", *zu)
    receive(X0, "gx", *x0)
    receive(Y0, "gy", *y0)

    def unpack_first(z, carry):
        u[0, z + 1, PAD - 1:PAD, :] = xr1[0, 0, z]
        u[0, z + 1, last:last + 1, :] = xr1[1, 0, z]
        return carry

    lax.fori_loop(0, depth, unpack_first, 0, unroll=UNROLL)

    def unpack_inputs(z, carry):
        for i in range(1, 4):
            fields[i][z + 1, PAD - 1:PAD, :] = xr1[0, i, z]
            fields[i][z + 1, last:last + 1, :] = xr1[1, i, z]
        k[z + 1, PAD - 1:PAD, :] = jnp.zeros((1, lanes), f32)
        k[z + 1, last:last + 1, :] = jnp.zeros((1, lanes), f32)
        return carry

    def shifts(field, packs, z, row):
        at = PAD + row
        mid = field[z + 1, at:at + ROWS, :]
        xm = field[z + 1, at - 1:at - 1 + ROWS, :]
        xp = field[z + 1, at + 1:at + 1 + ROWS, :]
        ym, yp = yshift(mid, packs, z, row)
        return mid, xm, xp, ym, yp

    base = me["gz"] * depth
    chunks = range(0, width, ROWS)

    ylo, yhi = zero8, zero8
    for row in chunks:
        rows = slice(row, row + ROWS)
        at = slice(PAD + row, PAD + row + ROWS)
        height = th[rows, :]
        packs = (yr1[0], yr1[1])

        def strain_step(z, carry):
            acc, lo, hi = carry
            up = u[0, z + 1, PAD + row + 1:PAD + row + 1 + ROWS, :]
            down = u[0, z + 1, PAD + row - 1:PAD + row - 1 + ROWS, :]
            ym, yp = yshift(u[1, z + 1, at, :], packs, z, row)
            div = 0.5 * (up - down) + 0.5 * (yp - ym) + 0.5 * (u[2, z + 2, at, :] - u[2, z, at, :])
            st = 0.3 * jnp.tanh(div)
            s[z + 1, at, :] = st
            if row == 0:
                xs2[0, z] = st[0:1, :]
            if row + ROWS == width:
                xs2[1, z] = st[ROWS - 1:ROWS, :]
            for g in range(ROWS // 8):
                lo, hi = pack(st[8 * g:8 * g + 8, :], z, row // 8 + g, lo, hi)
            acc = acc + jnp.where(base + z < height, 1.0 + st, 0.0)
            pre[z, rows, :] = acc
            return acc, lo, hi

        acc, ylo, yhi = lax.fori_loop(0, depth, strain_step, (jnp.zeros((ROWS, lanes), f32), ylo, yhi), unroll=UNROLL)
        tot[rows, :] = acc
    ys2[0], ys2[1] = yhi, ylo

    def column(off, at):
        return pltpu.make_async_remote_copy(
            src_ref=tot,
            dst_ref=cs.at[off - 1],
            send_sem=col_send.at[off - 1],
            recv_sem=col_recv.at[off - 1],
            device_id={"gz": lax.rem(me["gz"] + at, size["gz"])},
            device_id_type=MESH,
        )

    for off in range(1, size["gz"]):
        column(off, off).start()
    send(X2, "gx", *x2)
    send(Y2, "gy", *y2)
    send(ZS, "gz", *zs)

    receive(ZP, "gz", *zp)
    receive(X1, "gx", *x1)
    receive(Y1, "gy", *y1)
    lax.fori_loop(0, depth, unpack_inputs, 0, unroll=UNROLL)
    for row in chunks:
        rows = slice(row, row + ROWS)
        at = slice(PAD + row, PAD + row + ROWS)
        packs = [(yrr[0, 0], yrr[1, 0]), (yr1[0], yr1[1]), (yrr[0, 1], yrr[1, 1]), (yrr[0, 2], yrr[1, 2])]

        def lateral_step(z, carry):
            _, xm, xp, ym, yp = shifts(p, packs[3], z, row)
            grads = (xp - xm, yp - ym, p[z + 2, at, :] - p[z, at, :])
            for c in range(3):
                mid, xm, xp, ym, yp = shifts(u.at[c], packs[c], z, row)
                mech[c, z, rows, :] = xp + xm + yp + ym - 4.0 * mid - 0.5 * grads[c]
            return carry

        lax.fori_loop(0, depth, lateral_step, 0, unroll=UNROLL)

    loads[5].wait()

    def unloaded(zones, st, active):
        h = 1.0 + st
        perm = jnp.full(zones.shape, table[0], f32)
        for i in range(1, ZONES):
            perm = jnp.where(zones == i, table[i], perm)
        return perm * (h * h * h) * jnp.where(active, 0.001 + 0.999, 0.001)

    for row in chunks:
        rows = slice(row, row + ROWS)
        at = slice(PAD + row, PAD + row + ROWS)
        height = th[rows, :]

        def unloaded_step(z, carry):
            k[z + 1, at, :] = unloaded(zn[z + 1, rows, :], s[z + 1, at, :], base + z < height)
            return carry

        lax.fori_loop(0, depth, unloaded_step, 0, unroll=UNROLL)

    for off in range(1, size["gz"]):
        column(off, size["gz"] - off).wait_recv()

    def column_ends(rows):
        offset = jnp.zeros((ROWS, lanes), f32)
        total = tot[rows, :]
        for off in range(1, size["gz"]):
            piece = cs[off - 1, rows, :]
            offset = offset + piece * (me["gz"] >= off).astype(f32)
            total = total + piece
        return offset, total

    def permeability(free, burden):
        return free / (1.0 + 2.0 * burden)

    ylo, yhi = zero8, zero8
    for row in chunks:
        rows = slice(row, row + ROWS)
        at = slice(PAD + row, PAD + row + ROWS)
        offset, total = column_ends(rows)

        def kperm_step(z, carry):
            lo, hi = carry
            prefix = pre[z, rows, :] + offset
            heights[z, rows, :] = prefix / depth_total
            kp = permeability(k[z + 1, at, :], (total - prefix) / depth_total)
            k[z + 1, at, :] = kp
            if row == 0:
                xs3[0, z] = kp[0:1, :]
            if row + ROWS == width:
                xs3[1, z] = kp[ROWS - 1:ROWS, :]
            for g in range(ROWS // 8):
                lo, hi = pack(kp[8 * g:8 * g + 8, :], z, row // 8 + g, lo, hi)
            return lo, hi

        ylo, yhi = lax.fori_loop(0, depth, kperm_step, (ylo, yhi), unroll=UNROLL)

    ys3[0], ys3[1] = yhi, ylo
    send(X3, "gx", *x3)
    send(Y3, "gy", *y3)

    receive(ZS, "gz", *zs)
    receive(ZN, "gz", *zz)
    for row in chunks:
        rows = slice(row, row + ROWS)
        at = slice(PAD + row, PAD + row + ROWS)
        height = th[rows, :]
        offset, total = column_ends(rows)

        @pl.when(has("gz", 0))
        def _():
            free = unloaded(zn[0, rows, :], s[0, at, :], base - 1 < height)
            k[0, at, :] = permeability(free, (total - offset) / depth_total)

        @pl.when(has("gz", 1))
        def _():
            st = s[depth + 1, at, :]
            active = base + depth < height
            prefix = offset + tot[rows, :] + jnp.where(active, 1.0 + st, 0.0)
            free = unloaded(zn[depth + 1, rows, :], st, active)
            k[depth + 1, at, :] = permeability(free, (total - prefix) / depth_total)

    for row in chunks:
        rows = slice(row, row + ROWS)

        def flow_step(z, carry):
            ka, *ks = shifts(k, None, z, row)
            pa, *ps = shifts(p, None, z, row)
            out = jnp.zeros((ROWS, lanes), f32)
            twice = 2.0 * ka
            for kb, pb in zip(ks, ps):
                out = out + twice * kb / (ka + kb) * (pb - pa)
            flow[z, rows, :] = out
            return carry

        lax.fori_loop(0, depth, flow_step, 0, unroll=UNROLL)

    receive(ZL, "gz", *zl)
    receive(X2, "gx", *x2)
    receive(Y2, "gy", *y2)

    def unpack_strain(z, carry):
        s[z + 1, PAD - 1:PAD, :] = xr2[0, z]
        s[z + 1, last:last + 1, :] = xr2[1, z]
        return carry

    lax.fori_loop(0, depth, unpack_strain, 0, unroll=UNROLL)

    for row in chunks:
        rows = slice(row, row + ROWS)
        at = slice(PAD + row, PAD + row + ROWS)
        packs = (yr2[0], yr2[1])

        def faces(z):
            ka, kb = k[z, at, :], k[z + 1, at, :]
            hh = 2.0 + s[z, at, :] + s[z + 1, at, :]
            twice = 2.0 / hh
            cond = 2.0 * twice * (ka * kb) / (ka + kb)
            fluxes = [twice * (u[c, z + 1, at, :] - u[c, z, at, :]) for c in range(3)]
            return fluxes, cond * (p[z + 1, at, :] - p[z, at, :])

        def vertical_step(z, carry):
            below, flow_below = carry
            above, flow_above = faces(z + 1)
            mid, xm, xp, ym, yp = shifts(s, packs, z, row)
            flow[z, rows, :] = flow[z, rows, :] + (flow_above - flow_below) - mid
            grads = (xp - xm, yp - ym, s[z + 2, at, :] - s[z, at, :])
            for c in range(3):
                mech[c, z, rows, :] = mech[c, z, rows, :] + (above[c] - below[c]) + 0.25 * grads[c]
            return above, flow_above

        lax.fori_loop(0, depth, vertical_step, faces(0), unroll=UNROLL)

    receive(X3, "gx", *x3)
    receive(Y3, "gy", *y3)

    def crossing(ka, kb, pa, pb):
        return 2.0 * ka * kb / (ka + kb) * (pb - pa)

    turn = lambda face: pltpu.roll(face, 1, 1)
    side_lo = crossing(ys3[0], turn(yr3[0]), ysr[0, 2], turn(yrr[0, 2]))
    side_hi = crossing(turn(ys3[1]), yr3[1], turn(ysr[1, 2]), yrr[1, 2])
    first8, last8 = lane == 0, lane == lanes - 1

    def sides_step(z, carry):
        for side, row in ((0, 0), (1, width - 1)):
            out = crossing(xs3[side, z], xr3[side, z], xs1[side, 3, z], xr1[side, 3, z])
            flow[z, row:row + 1, :] = flow[z, row:row + 1, :] + out
        for g in range(groups):
            slot = z * groups + g
            lo = pltpu.roll(side_lo, lax.rem(lanes - slot, lanes), 1)
            hi = pltpu.roll(side_hi, lanes - 1 - slot, 1)
            rows = slice(8 * g, 8 * g + 8)
            flow[z, rows, :] = flow[z, rows, :] + jnp.where(first8, lo, jnp.where(last8, hi, 0.0))
        return carry

    lax.fori_loop(0, depth, sides_step, 0, unroll=UNROLL)

    for message, axis, srcs, dsts in pending:
        for side in (0, 1):
            @pl.when(has(axis, side))
            def _():
                copy(message, axis, side, srcs[side], dsts[1 - side], side).wait_send()
    for off in range(1, size["gz"]):
        column(off, off).wait_send()


def store(heights, flow, mech, heights_out, flow_out, mech_out, sem):
    pairs = ((mech, mech_out), (heights, heights_out), (flow, flow_out))
    copies = [pltpu.make_async_copy(src, dst, sem.at[i]) for i, (src, dst) in enumerate(pairs)]
    for copy in copies:
        copy.start()
    for copy in copies:
        copy.wait()


def local(counts, displacement, pressure, zone, perm_table, thickness):
    _, depth, width, lanes = displacement.shape
    f32 = jnp.float32
    tall = (depth + 2, width + 2 * PAD, lanes)
    row_face = lambda *lead: pltpu.VMEM((2, *lead, depth, 1, lanes), f32)
    lane_face = lambda *lead: pltpu.VMEM((2, *lead, 8, lanes), f32)
    hbm, vmem, smem = (pl.BlockSpec(memory_space=m) for m in (pl.ANY, pltpu.VMEM, pltpu.SMEM))
    others = max(counts[2] - 1, 1)
    inputs = [
        pltpu.with_memory_space_constraint(x, pltpu.HBM)
        for x in (displacement, pressure, zone, perm_table, thickness)
    ]
    fields = pl.pallas_call(
        functools.partial(kernel, counts),
        out_shape=(
            pltpu.VMEM(pressure.shape, f32),
            pltpu.VMEM(pressure.shape, f32),
            pltpu.VMEM(displacement.shape, f32),
        ),
        in_specs=[hbm, hbm, hbm, smem, hbm],
        out_specs=(vmem, vmem, vmem),
        scratch_shapes=[
            pltpu.VMEM((3, *tall), f32),
            pltpu.VMEM(tall, f32),
            pltpu.VMEM(tall, f32),
            pltpu.VMEM(tall, f32),
            pltpu.VMEM((depth + 2, width, lanes), jnp.int32),
            pltpu.VMEM((width, lanes), jnp.int32),
            pltpu.VMEM((depth, width, lanes), f32),
            pltpu.VMEM((width, lanes), f32),
            row_face(4), row_face(4), lane_face(), lane_face(), lane_face(3), lane_face(3),
            row_face(), row_face(), lane_face(), lane_face(),
            row_face(), row_face(), lane_face(), lane_face(),
            pltpu.VMEM((others, width, lanes), f32),
            pltpu.SemaphoreType.DMA((6,)),
            pltpu.SemaphoreType.DMA((MESSAGES, 2)),
            pltpu.SemaphoreType.DMA((MESSAGES, 2)),
            pltpu.SemaphoreType.DMA((others,)),
            pltpu.SemaphoreType.DMA((others,)),
        ],
        compiler_params=pltpu.CompilerParams(
            collective_id=0, has_side_effects=True, vmem_limit_bytes=40 * 2**20
        ),
    )(*inputs)
    return pl.pallas_call(
        store,
        out_shape=tuple(jax.ShapeDtypeStruct(x.shape, f32) for x in (pressure, pressure, displacement)),
        in_specs=[vmem] * 3,
        out_specs=(hbm,) * 3,
        scratch_shapes=[pltpu.SemaphoreType.DMA((3,))],
        compiler_params=pltpu.CompilerParams(vmem_limit_bytes=2**20),
    )(*[pltpu.with_memory_space_constraint(x, pltpu.VMEM) for x in fields])


def solution(mesh):
    counts = tuple(mesh.shape[axis] for axis in AXES)
    in_specs = (
        P(None, "gz", "gx", "gy"),
        P("gz", "gx", "gy"),
        P("gz", "gx", "gy"),
        P(),
        P("gx", "gy"),
    )
    out_specs = (P("gz", "gx", "gy"), P("gz", "gx", "gy"), P(None, "gz", "gx", "gy"))
    return jax.shard_map(
        functools.partial(local, counts), mesh=mesh, in_specs=in_specs, out_specs=out_specs, check_vma=False
    )
```

```python
import functools

import jax
import jax.numpy as jnp
from jax import lax
from jax.experimental import pallas as pl
from jax.experimental.pallas import tpu as pltpu
from jax.sharding import PartitionSpec as P

MESH = pl.DeviceIdType.MESH
ZONES = 8
AXES = ("gx", "gy", "gz")
PAD = 8
ROWS = 32
UNROLL = 8

X0, Y0, X1, Y1, ZU, ZL, ZP, ZN, X2, Y2, ZS, X3, Y3 = range(13)
MESSAGES = 13


def kernel(
    counts, disp, press, zone, table, thick, heights, flow, mech, lane_sides, row_sides,
    u, p, s, k, zn, th, pre, tot, xs1, xr1, ys1, yr1, ysr, yrr, xs2, xr2, ys2, yr2, xs3, xr3, ys3, yr3, cs,
    load_sem, send_sem, recv_sem, col_send, col_recv,
):
    depth, width = disp.shape[1], disp.shape[2]
    lanes = disp.shape[3]
    groups = width // 8
    last = PAD + width
    me = {axis: lax.axis_index(axis) for axis in AXES}
    size = dict(zip(AXES, counts))
    depth_total = depth * size["gz"]
    own = pl.ds(PAD, width)
    f32 = jnp.float32

    def has(axis, side):
        return me[axis] > 0 if side == 0 else me[axis] < size[axis] - 1

    def peer(axis, side):
        return {axis: me[axis] + (1 if side else -1)}

    loads = [
        pltpu.make_async_copy(disp.at[1], u.at[1, pl.ds(1, depth), own], load_sem.at[0]),
        pltpu.make_async_copy(disp.at[0], u.at[0, pl.ds(1, depth), own], load_sem.at[1]),
        pltpu.make_async_copy(disp.at[2], u.at[2, pl.ds(1, depth), own], load_sem.at[2]),
        pltpu.make_async_copy(press, p.at[pl.ds(1, depth), own], load_sem.at[3]),
        pltpu.make_async_copy(thick, th, load_sem.at[4]),
        pltpu.make_async_copy(zone, zn.at[pl.ds(1, depth)], load_sem.at[5]),
    ]
    for load in loads:
        load.start()

    barrier = pltpu.get_barrier_semaphore()
    partners = jnp.int32(size["gz"] - 1)
    for axis in ("gx", "gy"):
        for side in (0, 1):
            @pl.when(has(axis, side))
            def _():
                pl.semaphore_signal(barrier, inc=1, device_id=peer(axis, side), device_id_type=MESH)
            partners = partners + has(axis, side).astype(jnp.int32)
    for off in range(1, size["gz"]):
        pl.semaphore_signal(
            barrier, inc=1, device_id={"gz": lax.rem(me["gz"] + off, size["gz"])}, device_id_type=MESH
        )

    pending = []

    def copy(message, axis, side, src, dst, at):
        return pltpu.make_async_remote_copy(
            src_ref=src,
            dst_ref=dst,
            send_sem=send_sem.at[message, side],
            recv_sem=recv_sem.at[message, side],
            device_id=peer(axis, at),
            device_id_type=MESH,
        )

    def send(message, axis, srcs, dsts):
        for side in (0, 1):
            @pl.when(has(axis, side))
            def _():
                copy(message, axis, side, srcs[side], dsts[1 - side], side).start()
        pending.append((message, axis, srcs, dsts))

    def receive(message, axis, srcs, dsts):
        for side in (0, 1):
            @pl.when(has(axis, 1 - side))
            def _():
                copy(message, axis, side, srcs[side], dsts[1 - side], 1 - side).wait_recv()

    def clear(axis, refs):
        for side in (0, 1):
            @pl.when(jnp.logical_not(has(axis, side)))
            def _():
                for ref in refs[side]:
                    ref[...] = jnp.zeros(ref.shape, ref.dtype)

    def pair(ref):
        return (ref.at[0], ref.at[1])

    zu = ((disp.at[2, 0], disp.at[2, depth - 1]), (u.at[2, 0, own], u.at[2, depth + 1, own]))
    zl = (
        (disp.at[pl.ds(0, 2), 0], disp.at[pl.ds(0, 2), depth - 1]),
        (u.at[pl.ds(0, 2), 0, own], u.at[pl.ds(0, 2), depth + 1, own]),
    )
    zp = ((press.at[0], press.at[depth - 1]), (p.at[0, own], p.at[depth + 1, own]))
    zz = ((zone.at[0], zone.at[depth - 1]), (zn.at[0], zn.at[depth + 1]))
    zs = ((s.at[1, own], s.at[depth, own]), (s.at[0, own], s.at[depth + 1, own]))
    lane = lax.broadcasted_iota(jnp.int32, (8, lanes), 1)
    lane_r = lax.broadcasted_iota(jnp.int32, (ROWS, lanes), 1)
    first_lane, last_lane = lane_r == 0, lane_r == lanes - 1
    zero8 = jnp.zeros((8, lanes), f32)

    def pack(values, z, g, lo, hi):
        slot = z * groups + g
        turned = pltpu.roll(values, slot, 1)
        hi = jnp.where(lane == slot, turned, hi)
        lo = jnp.where(lane == lax.rem(slot + lanes - 1, lanes), turned, lo)
        return lo, hi

    def yshift(v, packs, z, row):
        if packs is None:
            below = jnp.where(first_lane, 0.0, pltpu.roll(v, 1, 1))
            return below, jnp.where(last_lane, 0.0, pltpu.roll(v, lanes - 1, 1))
        lo, hi = [], []
        lo_pack, hi_pack = packs
        for g in range(ROWS // 8):
            slot = z * groups + row // 8 + g
            lo.append(pltpu.roll(lo_pack, lax.rem(lanes + 1 - slot, lanes), 1))
            hi.append(pltpu.roll(hi_pack, lanes - 1 - slot, 1))
        lo, hi = jnp.concatenate(lo, axis=0), jnp.concatenate(hi, axis=0)
        below = jnp.where(first_lane, lo, pltpu.roll(v, 1, 1))
        above = jnp.where(last_lane, hi, pltpu.roll(v, lanes - 1, 1))
        return below, above

    fields = [u.at[0], u.at[1], u.at[2], p]

    def pack_first(z, carry):
        lo, hi = carry
        xs1[0, 0, z] = u[0, z + 1, PAD:PAD + 1, :]
        xs1[1, 0, z] = u[0, z + 1, last - 1:last, :]
        for g in range(groups):
            lo, hi = pack(u[1, z + 1, PAD + 8 * g:PAD + 8 * g + 8, :], z, g, lo, hi)
        return lo, hi

    loads[0].wait()
    loads[1].wait()
    lo, hi = lax.fori_loop(0, depth, pack_first, (zero8,) * 2, unroll=UNROLL)
    ys1[0] = hi
    ys1[1] = lo

    def part(ref, which):
        return (ref.at[0, which], ref.at[1, which])

    x0, y0 = (part(xs1, 0), part(xr1, 0)), (pair(ys1), pair(yr1))
    x1, y1 = (part(xs1, pl.ds(1, 3)), part(xr1, pl.ds(1, 3))), (pair(ysr), pair(yrr))
    pl.semaphore_wait(barrier, partners)
    send(ZU, "gz", *zu)
    send(X0, "gx", *x0)
    send(Y0, "gy", *y0)

    others = ((0, 0), (2, 1), (3, 2))

    def pack_inputs(z, accs):
        out = []
        for i in range(1, 4):
            xs1[0, i, z] = fields[i][z + 1, PAD:PAD + 1, :]
            xs1[1, i, z] = fields[i][z + 1, last - 1:last, :]
        for i, n in others:
            lo, hi = accs[2 * n:2 * n + 2]
            for g in range(groups):
                lo, hi = pack(fields[i][z + 1, PAD + 8 * g:PAD + 8 * g + 8, :], z, g, lo, hi)
            out += [lo, hi]
        return tuple(out)

    loads[2].wait()
    loads[3].wait()
    accs = lax.fori_loop(0, depth, pack_inputs, (zero8,) * 6, unroll=UNROLL)
    for i, n in others:
        ysr[0, n] = accs[2 * n + 1]
        ysr[1, n] = accs[2 * n]
    x2, y2 = (pair(xs2), pair(xr2)), (pair(ys2), pair(yr2))
    x3, y3 = (pair(xs3), pair(xr3)), (pair(ys3), pair(yr3))
    send(X1, "gx", *x1)
    send(Y1, "gy", *y1)
    send(ZL, "gz", *zl)
    send(ZP, "gz", *zp)
    send(ZN, "gz", *zz)

    clear("gx", [[xr.at[side] for xr in (xr1, xr2, xr3)] for side in (0, 1)])
    clear("gy", [[yr.at[side] for yr in (yr1, yrr, yr2, yr3)] for side in (0, 1)])
    edges = (0, depth + 1)
    clear("gz", [[u.at[:, z, own], p.at[z, own], s.at[z, own], k.at[z, own], zn.at[z]] for z in edges])
    loads[4].wait()

    receive(ZU, "gz", *zu)
    receive(X0, "gx", *x0)
    receive(Y0, "gy", *y0)

    def unpack_first(z, carry):
        u[0, z + 1, PAD - 1:PAD, :] = xr1[0, 0, z]
        u[0, z + 1, last:last + 1, :] = xr1[1, 0, z]
        return carry

    lax.fori_loop(0, depth, unpack_first, 0, unroll=UNROLL)

    def unpack_inputs(z, carry):
        for i in range(1, 4):
            fields[i][z + 1, PAD - 1:PAD, :] = xr1[0, i, z]
            fields[i][z + 1, last:last + 1, :] = xr1[1, i, z]
        k[z + 1, PAD - 1:PAD, :] = jnp.zeros((1, lanes), f32)
        k[z + 1, last:last + 1, :] = jnp.zeros((1, lanes), f32)
        return carry

    def shifts(field, packs, z, row):
        at = PAD + row
        mid = field[z + 1, at:at + ROWS, :]
        xm = field[z + 1, at - 1:at - 1 + ROWS, :]
        xp = field[z + 1, at + 1:at + 1 + ROWS, :]
        ym, yp = yshift(mid, packs, z, row)
        return mid, xm, xp, ym, yp

    base = me["gz"] * depth
    chunks = range(0, width, ROWS)

    ylo, yhi = zero8, zero8
    for row in chunks:
        rows = slice(row, row + ROWS)
        at = slice(PAD + row, PAD + row + ROWS)
        height = th[rows, :]
        packs = (yr1[0], yr1[1])

        def strain_step(z, carry):
            acc, lo, hi = carry
            up = u[0, z + 1, PAD + row + 1:PAD + row + 1 + ROWS, :]
            down = u[0, z + 1, PAD + row - 1:PAD + row - 1 + ROWS, :]
            ym, yp = yshift(u[1, z + 1, at, :], packs, z, row)
            div = 0.5 * (up - down) + 0.5 * (yp - ym) + 0.5 * (u[2, z + 2, at, :] - u[2, z, at, :])
            st = 0.3 * jnp.tanh(div)
            s[z + 1, at, :] = st
            if row == 0:
                xs2[0, z] = st[0:1, :]
            if row + ROWS == width:
                xs2[1, z] = st[ROWS - 1:ROWS, :]
            for g in range(ROWS // 8):
                lo, hi = pack(st[8 * g:8 * g + 8, :], z, row // 8 + g, lo, hi)
            acc = acc + jnp.where(base + z < height, 1.0 + st, 0.0)
            pre[z, rows, :] = acc
            return acc, lo, hi

        acc, ylo, yhi = lax.fori_loop(0, depth, strain_step, (jnp.zeros((ROWS, lanes), f32), ylo, yhi), unroll=UNROLL)
        tot[rows, :] = acc
    ys2[0], ys2[1] = yhi, ylo

    def column(off, at):
        return pltpu.make_async_remote_copy(
            src_ref=tot,
            dst_ref=cs.at[off - 1],
            send_sem=col_send.at[off - 1],
            recv_sem=col_recv.at[off - 1],
            device_id={"gz": lax.rem(me["gz"] + at, size["gz"])},
            device_id_type=MESH,
        )

    for off in range(1, size["gz"]):
        column(off, off).start()
    send(X2, "gx", *x2)
    send(Y2, "gy", *y2)
    send(ZS, "gz", *zs)

    receive(ZP, "gz", *zp)
    receive(X1, "gx", *x1)
    receive(Y1, "gy", *y1)
    lax.fori_loop(0, depth, unpack_inputs, 0, unroll=UNROLL)
    for row in chunks:
        rows = slice(row, row + ROWS)
        at = slice(PAD + row, PAD + row + ROWS)
        packs = [(yrr[0, 0], yrr[1, 0]), (yr1[0], yr1[1]), (yrr[0, 1], yrr[1, 1]), (yrr[0, 2], yrr[1, 2])]

        def lateral_step(z, carry):
            _, xm, xp, ym, yp = shifts(p, packs[3], z, row)
            grads = (xp - xm, yp - ym, p[z + 2, at, :] - p[z, at, :])
            for c in range(3):
                mid, xm, xp, ym, yp = shifts(u.at[c], packs[c], z, row)
                mech[c, z, rows, :] = xp + xm + yp + ym - 4.0 * mid - 0.5 * grads[c]
            return carry

        lax.fori_loop(0, depth, lateral_step, 0, unroll=UNROLL)

    loads[5].wait()

    def unloaded(zones, st, active):
        h = 1.0 + st
        perm = jnp.full(zones.shape, table[0], f32)
        for i in range(1, ZONES):
            perm = jnp.where(zones == i, table[i], perm)
        return perm * (h * h * h) * jnp.where(active, 0.001 + 0.999, 0.001)

    for row in chunks:
        rows = slice(row, row + ROWS)
        at = slice(PAD + row, PAD + row + ROWS)
        height = th[rows, :]

        def unloaded_step(z, carry):
            k[z + 1, at, :] = unloaded(zn[z + 1, rows, :], s[z + 1, at, :], base + z < height)
            return carry

        lax.fori_loop(0, depth, unloaded_step, 0, unroll=UNROLL)

    for off in range(1, size["gz"]):
        column(off, size["gz"] - off).wait_recv()

    def column_ends(rows):
        offset = jnp.zeros((ROWS, lanes), f32)
        total = tot[rows, :]
        for off in range(1, size["gz"]):
            piece = cs[off - 1, rows, :]
            offset = offset + piece * (me["gz"] >= off).astype(f32)
            total = total + piece
        return offset, total

    def permeability(free, burden):
        return free / (1.0 + 2.0 * burden)

    ylo, yhi = zero8, zero8
    for row in chunks:
        rows = slice(row, row + ROWS)
        at = slice(PAD + row, PAD + row + ROWS)
        offset, total = column_ends(rows)

        def kperm_step(z, carry):
            lo, hi = carry
            prefix = pre[z, rows, :] + offset
            heights[z, rows, :] = prefix / depth_total
            kp = permeability(k[z + 1, at, :], (total - prefix) / depth_total)
            k[z + 1, at, :] = kp
            if row == 0:
                xs3[0, z] = kp[0:1, :]
            if row + ROWS == width:
                xs3[1, z] = kp[ROWS - 1:ROWS, :]
            for g in range(ROWS // 8):
                lo, hi = pack(kp[8 * g:8 * g + 8, :], z, row // 8 + g, lo, hi)
            return lo, hi

        ylo, yhi = lax.fori_loop(0, depth, kperm_step, (ylo, yhi), unroll=UNROLL)

    ys3[0], ys3[1] = yhi, ylo
    send(X3, "gx", *x3)
    send(Y3, "gy", *y3)

    receive(ZS, "gz", *zs)
    receive(ZN, "gz", *zz)
    for row in chunks:
        rows = slice(row, row + ROWS)
        at = slice(PAD + row, PAD + row + ROWS)
        height = th[rows, :]
        offset, total = column_ends(rows)

        @pl.when(has("gz", 0))
        def _():
            free = unloaded(zn[0, rows, :], s[0, at, :], base - 1 < height)
            k[0, at, :] = permeability(free, (total - offset) / depth_total)

        @pl.when(has("gz", 1))
        def _():
            st = s[depth + 1, at, :]
            active = base + depth < height
            prefix = offset + tot[rows, :] + jnp.where(active, 1.0 + st, 0.0)
            free = unloaded(zn[depth + 1, rows, :], st, active)
            k[depth + 1, at, :] = permeability(free, (total - prefix) / depth_total)

    for row in chunks:
        rows = slice(row, row + ROWS)

        def flow_step(z, carry):
            ka, *ks = shifts(k, None, z, row)
            pa, *ps = shifts(p, None, z, row)
            out = jnp.zeros((ROWS, lanes), f32)
            twice = 2.0 * ka
            for kb, pb in zip(ks, ps):
                out = out + twice * kb / (ka + kb) * (pb - pa)
            flow[z, rows, :] = out
            return carry

        lax.fori_loop(0, depth, flow_step, 0, unroll=UNROLL)

    receive(ZL, "gz", *zl)
    receive(X2, "gx", *x2)
    receive(Y2, "gy", *y2)

    def unpack_strain(z, carry):
        s[z + 1, PAD - 1:PAD, :] = xr2[0, z]
        s[z + 1, last:last + 1, :] = xr2[1, z]
        return carry

    lax.fori_loop(0, depth, unpack_strain, 0, unroll=UNROLL)

    for row in chunks:
        rows = slice(row, row + ROWS)
        at = slice(PAD + row, PAD + row + ROWS)
        packs = (yr2[0], yr2[1])

        def faces(z):
            ka, kb = k[z, at, :], k[z + 1, at, :]
            hh = 2.0 + s[z, at, :] + s[z + 1, at, :]
            twice = 2.0 / hh
            cond = 2.0 * twice * (ka * kb) / (ka + kb)
            fluxes = [twice * (u[c, z + 1, at, :] - u[c, z, at, :]) for c in range(3)]
            return fluxes, cond * (p[z + 1, at, :] - p[z, at, :])

        def vertical_step(z, carry):
            below, flow_below = carry
            above, flow_above = faces(z + 1)
            mid, xm, xp, ym, yp = shifts(s, packs, z, row)
            flow[z, rows, :] = flow[z, rows, :] + (flow_above - flow_below) - mid
            grads = (xp - xm, yp - ym, s[z + 2, at, :] - s[z, at, :])
            for c in range(3):
                mech[c, z, rows, :] = mech[c, z, rows, :] + (above[c] - below[c]) + 0.25 * grads[c]
            return above, flow_above

        lax.fori_loop(0, depth, vertical_step, faces(0), unroll=UNROLL)

    receive(X3, "gx", *x3)
    receive(Y3, "gy", *y3)

    def crossing(ka, kb, pa, pb):
        return 2.0 * ka * kb / (ka + kb) * (pb - pa)

    turn = lambda face: pltpu.roll(face, 1, 1)
    lane_sides[0] = crossing(ys3[0], turn(yr3[0]), ysr[0, 2], turn(yrr[0, 2]))
    lane_sides[1] = crossing(turn(ys3[1]), yr3[1], turn(ysr[1, 2]), yrr[1, 2])

    def sides_step(z, carry):
        for side in (0, 1):
            row_sides[side, z] = crossing(xs3[side, z], xr3[side, z], xs1[side, 3, z], xr1[side, 3, z])
        return carry

    lax.fori_loop(0, depth, sides_step, 0, unroll=UNROLL)

    for message, axis, srcs, dsts in pending:
        for side in (0, 1):
            @pl.when(has(axis, side))
            def _():
                copy(message, axis, side, srcs[side], dsts[1 - side], side).wait_send()
    for off in range(1, size["gz"]):
        column(off, off).wait_send()


def store(heights, flow, mech, lane_sides, row_sides, heights_out, flow_out, mech_out, whole, sem):
    depth, width, lanes = whole.shape
    groups = width // 8
    copies = [
        pltpu.make_async_copy(mech, mech_out, sem.at[0]),
        pltpu.make_async_copy(heights, heights_out, sem.at[1]),
    ]
    for copy in copies:
        copy.start()
    lane = lax.broadcasted_iota(jnp.int32, (8, lanes), 1)
    first, last = lane == 0, lane == lanes - 1
    side_lo, side_hi = lane_sides[0], lane_sides[1]

    def step(z, carry):
        for g in range(groups):
            slot = z * groups + g
            lo = pltpu.roll(side_lo, lax.rem(lanes - slot, lanes), 1)
            hi = pltpu.roll(side_hi, lanes - 1 - slot, 1)
            rows = slice(8 * g, 8 * g + 8)
            whole[z, rows, :] = flow[z, rows, :] + jnp.where(first, lo, jnp.where(last, hi, 0.0))
        for side, row in ((0, 0), (1, width - 1)):
            whole[z, row:row + 1, :] = whole[z, row:row + 1, :] + row_sides[side, z]
        return carry

    half = depth // 2
    for part in range(2):
        lax.fori_loop(part * half, (part + 1) * half, step, 0, unroll=4)
        layers = pl.ds(part * half, half)
        copy = pltpu.make_async_copy(whole.at[layers], flow_out.at[layers], sem.at[2 + part])
        copy.start()
        copies.append(copy)
    for copy in copies:
        copy.wait()


def local(counts, displacement, pressure, zone, perm_table, thickness):
    _, depth, width, lanes = displacement.shape
    f32 = jnp.float32
    tall = (depth + 2, width + 2 * PAD, lanes)
    row_face = lambda *lead: pltpu.VMEM((2, *lead, depth, 1, lanes), f32)
    lane_face = lambda *lead: pltpu.VMEM((2, *lead, 8, lanes), f32)
    hbm, vmem, smem = (pl.BlockSpec(memory_space=m) for m in (pl.ANY, pltpu.VMEM, pltpu.SMEM))
    others = max(counts[2] - 1, 1)
    inputs = [
        pltpu.with_memory_space_constraint(x, pltpu.HBM)
        for x in (displacement, pressure, zone, perm_table, thickness)
    ]
    fields = pl.pallas_call(
        functools.partial(kernel, counts),
        out_shape=(
            pltpu.VMEM(pressure.shape, f32),
            pltpu.VMEM(pressure.shape, f32),
            pltpu.VMEM(displacement.shape, f32),
            pltpu.VMEM((2, 8, lanes), f32),
            pltpu.VMEM((2, depth, 1, lanes), f32),
        ),
        in_specs=[hbm, hbm, hbm, smem, hbm],
        out_specs=(vmem,) * 5,
        scratch_shapes=[
            pltpu.VMEM((3, *tall), f32),
            pltpu.VMEM(tall, f32),
            pltpu.VMEM(tall, f32),
            pltpu.VMEM(tall, f32),
            pltpu.VMEM((depth + 2, width, lanes), jnp.int32),
            pltpu.VMEM((width, lanes), jnp.int32),
            pltpu.VMEM((depth, width, lanes), f32),
            pltpu.VMEM((width, lanes), f32),
            row_face(4), row_face(4), lane_face(), lane_face(), lane_face(3), lane_face(3),
            row_face(), row_face(), lane_face(), lane_face(),
            row_face(), row_face(), lane_face(), lane_face(),
            pltpu.VMEM((others, width, lanes), f32),
            pltpu.SemaphoreType.DMA((6,)),
            pltpu.SemaphoreType.DMA((MESSAGES, 2)),
            pltpu.SemaphoreType.DMA((MESSAGES, 2)),
            pltpu.SemaphoreType.DMA((others,)),
            pltpu.SemaphoreType.DMA((others,)),
        ],
        compiler_params=pltpu.CompilerParams(
            collective_id=0, has_side_effects=True, vmem_limit_bytes=40 * 2**20
        ),
    )(*inputs)
    return pl.pallas_call(
        store,
        out_shape=tuple(jax.ShapeDtypeStruct(x.shape, f32) for x in (pressure, pressure, displacement)),
        in_specs=[vmem] * 5,
        out_specs=(hbm,) * 3,
        scratch_shapes=[pltpu.VMEM(pressure.shape, f32), pltpu.SemaphoreType.DMA((4,))],
        compiler_params=pltpu.CompilerParams(vmem_limit_bytes=4 * 2**20),
    )(*[pltpu.with_memory_space_constraint(x, pltpu.VMEM) for x in fields])


def solution(mesh):
    counts = tuple(mesh.shape[axis] for axis in AXES)
    in_specs = (
        P(None, "gz", "gx", "gy"),
        P("gz", "gx", "gy"),
        P("gz", "gx", "gy"),
        P(),
        P("gx", "gy"),
    )
    out_specs = (P("gz", "gx", "gy"), P("gz", "gx", "gy"), P(None, "gz", "gx", "gy"))
    return jax.shard_map(
        functools.partial(local, counts), mesh=mesh, in_specs=in_specs, out_specs=out_specs, check_vma=False
    )
```
